512 devices in a mesh: seq: 64 (over z, y_hi, core), mp: 8 (over y_lo, x).
Axes of the slice: x: 4, y: 4 (y_hi: 2, y_lo: 2; y = y_hi * 2 + y_lo), z: 16, core: 2. Of those that a mesh axis runs over, the one named last changes fastest.
Arguments:
- query: bfloat16 [1, 64, 64, 1024], P(None, 'seq', None, 'mp'), may hold values from -6 to 6
- keys: bfloat16 [1, 64, 64, 1024], P(None, 'seq', None, 'mp'), may hold values from -6 to 6
- values: bfloat16 [1, 64, 64, 1024], P(None, 'seq', None, 'mp'), may hold values from -6 to 6
- resid: bfloat16 [1, 64, 64, 1920], P(None, 'seq', 'mp'), may hold values from -4 to 4
- out_weight: bfloat16 [1024, 1920], P('mp'), may hold values from -0.1875 to 0.1875
- norm_gain: float32 [1920], replicated, may hold values from 0.1 to 1.9
- norm_bias: float32 [1920], replicated, may hold values from -3 to 3
- deconv1_weight: bfloat16 [384, 4, 4, 1920], P('mp'), may hold values from -0.0625 to 0.0625
- deconv1_bias: float32 [384], P('mp'), may hold values from -3 to 3
- deconv2_weight: bfloat16 [384, 4, 4, 384], P('mp'), may hold values from -0.15625 to 0.15625
- deconv2_bias: float32 [384], P('mp'), may hold values from -3 to 3
- final_weight: bfloat16 [384, 308], replicated, may hold values from -0.3125 to 0.3125
- final_bias: float32 [308], replicated, may hold values from -3 to 3
Outputs:
- heatmaps: bfloat16 [1, 256, 256, 308], P(None, 'seq', 'mp')
The draws below stay inside these ranges and needn't reach their ends.
All inputs are finite; a program needn't handle non-finite values.
Results may differ from the reference program's by a relative error of at most 0.012.
Values may be sent and summed in bfloat16 or wider, within the bound.
A program may use at most 64 MiB of HBM per device.

```python
import jax
import jax.numpy as jnp
from jax import lax

D = 1920
HEADS = 16
HEAD_DIM = 64
CHANNELS = 384
KEYPOINTS = 308
GRID = 64
FRAMES = 1


def draw_query(key, part):
    base = jax.random.normal(jax.random.fold_in(key, 11), (FRAMES, GRID, GRID, HEADS * HEAD_DIM), jnp.float32) * 1.4
    base = jnp.clip(base, -6.0, 6.0)
    return base.astype(jnp.bfloat16)


def draw_keys(key, part):
    base = jax.random.normal(jax.random.fold_in(key, 12), (FRAMES, GRID, GRID, HEADS * HEAD_DIM), jnp.float32) * 1.4
    base = jnp.clip(base, -6.0, 6.0)
    return base.astype(jnp.bfloat16)


def levels(own_key, shape, split, smallest, high):
    gain, own = 1.0, jax.random.fold_in(own_key, 6)
    for dim, shards_of in split:
        draws = jnp.exp(jax.random.uniform(jax.random.fold_in(own, dim), (shards_of,), jnp.float32, smallest / len(split), high / len(split)))
        gain = gain * jnp.repeat(draws, shape[dim] // shards_of).reshape([-1 if axis == dim else 1 for axis in range(len(shape))])
    return gain


def gaussian(stream_key, shape, deviation, bound, shards=(), dtype=jnp.bfloat16):
    entries = deviation * jax.random.normal(stream_key, shape, jnp.float32)
    if shards:
        entries = entries * levels(stream_key, shape, shards, -0.22, 0.18)
    return jnp.clip(entries, -bound, bound).astype(dtype)


def setup_inputs(seed: int = 0) -> dict:
    seeds = jax.random.split(jax.random.key(seed), 14)
    query = draw_query(jax.random.fold_in(seeds[13], 71), 0)
    keys = draw_keys(jax.random.fold_in(seeds[13], 71), 0)
    values = gaussian(seeds[2], (FRAMES, GRID, GRID, HEADS * HEAD_DIM), 1.0, 6.0, ((1, 64), (3, 8)))
    resid = gaussian(seeds[3], (FRAMES, GRID, GRID, D), 0.3, 4.0, ((1, 64), (2, 8)))
    out_weight = gaussian(seeds[4], (HEADS * HEAD_DIM, D), (HEADS * HEAD_DIM) ** -0.5, 0.1875, ((0, 8),))
    norm_gain = jnp.clip(1.0 + 0.18 * jax.random.normal(seeds[5], (D,), jnp.float32), 0.1, 1.9)
    norm_bias = gaussian(seeds[6], (D,), 0.5, 3.0, (), jnp.float32)
    deconv1_weight = gaussian(seeds[7], (CHANNELS, 4, 4, D), (4 * D) ** -0.5, 0.0625, ((0, 8),))
    deconv1_bias = gaussian(seeds[8], (CHANNELS,), 0.5, 3.0, ((0, 8),), jnp.float32)
    deconv2_weight = gaussian(seeds[9], (CHANNELS, 4, 4, CHANNELS), (4 * CHANNELS) ** -0.5, 0.15625, ((0, 8),))
    deconv2_bias = gaussian(seeds[10], (CHANNELS,), 0.5, 3.0, ((0, 8),), jnp.float32)
    final_weight = gaussian(seeds[11], (CHANNELS, KEYPOINTS), CHANNELS ** -0.5, 0.3125)
    final_bias = gaussian(seeds[12], (KEYPOINTS,), 0.5, 3.0, (), jnp.float32)
    return {"query": query, "keys": keys, "values": values, "resid": resid, "out_weight": out_weight, "norm_gain": norm_gain, "norm_bias": norm_bias, "deconv1_weight": deconv1_weight, "deconv1_bias": deconv1_bias, "deconv2_weight": deconv2_weight, "deconv2_bias": deconv2_bias, "final_weight": final_weight, "final_bias": final_bias}


TAP_TABLE = (((1, 1), (0, 3)), ((2, 0), (1, 2)))
EPSILON = 1e-06

def tap_product(window, weight, kernel_row, kernel_col):
    tap = weight[:, kernel_row, kernel_col, :]
    return lax.dot_general(window, tap, (((3,), (1,)), ((), ())), preferred_element_type=jnp.float32)

def half_rows(padded, weight, tap_pairs, first_row, row_count):
    col_count = padded.shape[2] - 2
    halves = []
    for col_parity in range(2):
        summed = None
        for pad_row, kernel_row in tap_pairs:
            for pad_col, kernel_col in TAP_TABLE[col_parity]:
                window = padded[:, first_row + pad_row:first_row + pad_row + row_count, pad_col:pad_col + col_count, :]
                product = tap_product(window, weight, kernel_row, kernel_col)
                summed = product if summed is None else summed + product
        halves.append(summed)
    stacked = jnp.stack(halves, axis=3)
    return stacked.reshape(stacked.shape[0], row_count, 2 * col_count, stacked.shape[-1])

def upsample(padded, weight, row_count):
    even_rows = half_rows(padded, weight, TAP_TABLE[0], 0, row_count)
    odd_rows = half_rows(padded, weight, TAP_TABLE[1], 0, row_count)
    stacked = jnp.stack([even_rows, odd_rows], axis=2)
    return stacked.reshape(stacked.shape[0], 2 * row_count, stacked.shape[3], stacked.shape[4])

def pad_grid(field):
    return jnp.pad(field, ((0, 0), (1, 1), (1, 1), (0, 0)))

def layer_norm(stream, norm_gain, norm_bias):
    center = lax.optimization_barrier(jnp.mean(stream, axis=-1, keepdims=True))
    shifted = stream - center
    variance = lax.optimization_barrier(jnp.mean(shifted * shifted, axis=-1, keepdims=True))
    return (shifted * lax.rsqrt(variance + EPSILON) * norm_gain + norm_bias).astype(jnp.bfloat16)

def reference(query, keys, values, resid, out_weight, norm_gain, norm_bias, deconv1_weight, deconv1_bias, deconv2_weight, deconv2_bias, final_weight, final_bias):
    token_count = GRID * GRID
    score_scale = HEAD_DIM ** (-0.5)

    def by_head(field):
        return jnp.transpose(field.reshape(FRAMES, token_count, HEADS, HEAD_DIM), (2, 0, 1, 3))

    def one_head(operands):
        query_head, key_head, value_head = operands
        scores = jnp.einsum('fqd,fkd->fqk', query_head.astype(jnp.float32), key_head.astype(jnp.float32), precision=lax.Precision.HIGHEST) * score_scale
        row_max = lax.optimization_barrier(jnp.max(scores, axis=-1, keepdims=True))
        exps = jnp.exp(scores - row_max)
        denominator = lax.optimization_barrier(jnp.sum(exps, axis=-1, keepdims=True))
        weights = lax.optimization_barrier(exps.astype(jnp.bfloat16))
        mixed = jnp.einsum('fqk,fkd->fqd', weights.astype(jnp.float32), value_head.astype(jnp.float32), precision=lax.Precision.HIGHEST)
        return (mixed / denominator).astype(jnp.bfloat16)
    attended = lax.map(one_head, (by_head(query), by_head(keys), by_head(values)))
    attended = jnp.transpose(attended, (1, 2, 0, 3)).reshape(FRAMES, GRID, GRID, HEADS * HEAD_DIM)
    stream = resid.astype(jnp.float32) + jnp.dot(attended, out_weight, preferred_element_type=jnp.float32)
    normed = layer_norm(stream, norm_gain, norm_bias)
    hidden_one = jnp.maximum(upsample(pad_grid(normed), deconv1_weight, GRID) + deconv1_bias, 0.0).astype(jnp.bfloat16)
    hidden_two = jnp.maximum(upsample(pad_grid(hidden_one), deconv2_weight, 2 * GRID) + deconv2_bias, 0.0).astype(jnp.bfloat16)
    return (jnp.dot(hidden_two, final_weight, preferred_element_type=jnp.float32) + final_bias).astype(jnp.bfloat16)
```

```python
import jax
import jax.numpy as jnp
from jax import lax
from jax.experimental import pallas as pl
from jax.experimental.pallas import tpu as pltpu
from jax.sharding import PartitionSpec as P

EPSILON = 1e-06
MESH = pl.DeviceIdType.MESH
F32 = jnp.float32
BF16 = jnp.bfloat16
ROWS = 64
COLS = 64
PEERS = 8
LAYERS = 16
CHANNELS = 48
TAPS = (1, 2, 3, 0)
CHUNK = 8


def nt(a, b):
    return lax.dot_general(a, b, (((1,), (1,)), ((), ())), preferred_element_type=F32)


def nn(a, b):
    return lax.dot_general(a, b, (((1,), (0,)), ((), ())), preferred_element_type=F32)


def shifted(field):
    row = lax.broadcasted_iota(jnp.int32, field.shape, 0) & (COLS - 1)
    lane = lax.broadcasted_iota(jnp.int32, field.shape, 1) & 127
    before = jnp.where(row == 0, 0.0, pltpu.roll(field, 1, 0))
    after = jnp.where(row == COLS - 1, 0.0, pltpu.roll(field, field.shape[0] - 1, 0))
    return jnp.where(lane < CHANNELS, before, after)


def body(
    q_ref, k_ref, v_ref, resid_ref, wo_ref, gain_ref, shift_ref, w1_ref, b1_ref, w2_ref, b2_ref, wf_ref, bf_ref,
    out_ref,
    kv, other, qb, qsend, asend, arecv, scores, part, got, normed, halo1s, halo1r, one, halo2s, halo2r, two, tiles,
    pair_s, pair_r, right_s, right_r, left_s, left_r, mp_s, mp_r, halo_s, halo_r,
):
    s = lax.axis_index("seq")
    m = lax.axis_index("mp")
    core = lax.rem(s, 2)
    y = lax.rem(lax.div(s, 2), 2)
    z = lax.div(s, 4)

    def seq_at(zz, yy, cc):
        return zz * 4 + yy * 2 + cc

    mate = seq_at(z, y, 1 - core)
    across = seq_at(z, 1 - y, core)
    diagonal = seq_at(z, 1 - y, 1 - core)
    z_up = lax.rem(s + 4, ROWS)
    z_down = lax.rem(s + ROWS - 4, ROWS)
    row_up = lax.rem(s + 1, ROWS)
    row_down = lax.rem(s + ROWS - 1, ROWS)

    barrier = pltpu.get_barrier_semaphore()
    greeted = [(mate, m), (across, m), (diagonal, m), (z_up, m), (z_down, m), (row_up, m), (row_down, m)]
    greeted += [(s, lax.rem(m + d, PEERS)) for d in range(1, PEERS)]
    for device in greeted:
        pl.semaphore_signal(barrier, inc=1, device_id=device, device_id_type=MESH)

    lane = lax.broadcasted_iota(jnp.int32, (COLS, 128), 1)
    low = lane < 64
    k = k_ref[...].astype(F32)
    v = v_ref[...].astype(F32)
    q = q_ref[...].astype(F32) * 0.125
    first = jnp.where(low, k, pltpu.roll(v, 64, 1))
    second = jnp.where(low, pltpu.roll(k, 64, 1), v)
    q_first = jnp.where(low, q, 0.0)
    q_second = jnp.where(low, pltpu.roll(q, 64, 1), 0.0)
    is_first = core == 0
    kv[s] = jnp.where(is_first, first, second).astype(BF16)
    other[...] = jnp.where(is_first, second, first).astype(BF16)
    qb[core] = jnp.where(is_first, q_first, q_second).astype(BF16)
    qsend[...] = jnp.where(is_first, q_second, q_first).astype(BF16)

    pl.semaphore_wait(barrier, len(greeted))

    def send(src, dst, ssem, rsem, device):
        return pltpu.make_async_remote_copy(
            src_ref=src, dst_ref=dst, send_sem=ssem, recv_sem=rsem, device_id=device, device_id_type=MESH
        )

    def piece(layer, p):
        yy = y if p < 2 else 1 - y
        cc = core if p % 2 == 0 else 1 - core
        return seq_at(layer, yy, cc)

    def right(t, p):
        block = kv.at[piece(lax.rem(z - t + LAYERS, LAYERS), p)]
        return send(block, block, right_s.at[t, p], right_r.at[t, p], (z_up, m))

    def left(t, p):
        block = kv.at[piece(lax.rem(z + t, LAYERS), p)]
        return send(block, block, left_s.at[t, p], left_r.at[t, p], (z_down, m))

    right(0, 0).start()
    left(0, 0).start()
    pair = [
        None,
        send(other, kv.at[s], pair_s.at[1], pair_r.at[1], (mate, m)),
        send(kv.at[s], kv.at[s], pair_s.at[2], pair_r.at[2], (across, m)),
        send(other, kv.at[s], pair_s.at[3], pair_r.at[3], (diagonal, m)),
        send(qsend, qb.at[core], pair_s.at[0], pair_r.at[0], (mate, m)),
    ]
    for p in (1, 2, 3, 4):
        pair[p].start()
    for p in (1, 2, 3):
        pair[p].wait_recv()
        right(0, p).start()
        left(0, p).start()

    def ring(t, carry):
        for p in range(4):
            right(t - 1, p).wait_recv()
            right(t, p).start()
            left(t - 1, p).wait_recv()
            left(t, p).start()
        return carry

    lax.fori_loop(1, 7, ring, 0)
    for p in range(4):
        right(6, p).wait_recv()
        right(7, p).start()
    for p in range(4):
        left(6, p).wait_recv()
    pair[4].wait_recv()
    for p in range(4):
        right(7, p).wait_recv()

    queries = qb[...].reshape(2 * COLS, 128)

    def score(j, best):
        block = kv[pl.ds(j * CHUNK, CHUNK)].reshape(CHUNK * COLS, 128)
        fresh = nt(queries, block)
        scores[j] = fresh
        return jnp.maximum(best, jnp.max(fresh, axis=1, keepdims=True))

    top = lax.fori_loop(0, ROWS // CHUNK, score, jnp.full((2 * COLS, 1), -jnp.inf, F32))

    def mix(j, carry):
        total, mixed = carry
        exps = jnp.exp(scores[j] - top)
        block = kv[pl.ds(j * CHUNK, CHUNK)].reshape(CHUNK * COLS, 128)
        return total + jnp.sum(exps, axis=1, keepdims=True), mixed + nn(exps.astype(BF16), block)

    total, mixed = lax.fori_loop(
        0, ROWS // CHUNK, mix, (jnp.zeros((2 * COLS, 1), F32), jnp.zeros((2 * COLS, 128), F32))
    )
    attended = mixed / total
    placed = jnp.where(is_first, jnp.where(low, pltpu.roll(attended[:COLS], 64, 1), 0.0), jnp.where(low, 0.0, attended[:COLS]))
    placed_too = jnp.where(is_first, jnp.where(low, pltpu.roll(attended[COLS:], 64, 1), 0.0), jnp.where(low, 0.0, attended[COLS:]))
    asend[...] = jnp.where(is_first, placed_too, placed).astype(BF16)
    swap = send(asend, arecv, pair_s.at[4], pair_r.at[4], (mate, m))
    swap.start()
    mine = jnp.where(is_first, placed, placed_too).astype(BF16)
    swap.wait_recv()
    rows = (mine.astype(F32) + arecv[...].astype(F32)).astype(BF16)

    def exchange(phase, source, target):
        copies = []
        for d in range(1, PEERS):
            peer = lax.rem(m + d, PEERS)
            copies.append(send(source(peer), target, mp_s.at[phase, d], mp_r.at[phase, d], (s, peer)))
        for copy in copies:
            copy.start()
        return copies

    def arrived(copies):
        for copy in copies:
            copy.wait_recv()

    part[...] = nn(rows, wo_ref[...]).reshape(PEERS, 8, -1).astype(BF16)
    sums = exchange(0, lambda peer: part.at[peer], got.at[m])
    stream = resid_ref[...].astype(F32) + part[m].astype(F32)
    got[m] = jnp.zeros(got.shape[1:], BF16)
    arrived(sums)
    for j in range(PEERS):
        stream = stream + got[j].astype(F32)
    center = jnp.mean(stream, axis=1, keepdims=True)
    apart = stream - center
    variance = jnp.mean(apart * apart, axis=1, keepdims=True)
    normed[m] = (apart * lax.rsqrt(variance + EPSILON) * gain_ref[...] + shift_ref[...]).astype(BF16)
    norms = exchange(1, lambda peer: normed.at[m], normed.at[m])
    arrived(norms)
    tokens = normed[...].astype(F32).reshape(COLS, -1).astype(BF16)

    def first_block(i):
        return nt(tokens, w1_ref[pl.ds(i * 256, 256), :])

    crossing = first_block(2) + shifted(first_block(3))
    halo1s[0] = crossing[:, :128]
    halo1s[1] = crossing[:, 128:]
    to_up = send(halo1s.at[0], halo1r.at[0], halo_s.at[0], halo_r.at[0], (row_up, m))
    to_down = send(halo1s.at[1], halo1r.at[1], halo_s.at[1], halo_r.at[1], (row_down, m))
    to_up.start()
    to_down.start()
    inside = first_block(0) + shifted(first_block(1))
    to_up.wait_recv()
    to_down.wait_recv()
    upper = inside[:, :128] + jnp.where(s > 0, halo1r[0], 0.0)
    lower = inside[:, 128:] + jnp.where(s < ROWS - 1, halo1r[1], 0.0)
    one[m, 0] = jnp.maximum(upper + b1_ref[...], 0.0).astype(BF16)
    one[m, 1] = jnp.maximum(lower + b1_ref[...], 0.0).astype(BF16)
    ones = exchange(2, lambda peer: one.at[m], one.at[m])
    arrived(ones)
    cells = jnp.concatenate([one[j].reshape(2 * COLS, 128) for j in range(PEERS)], axis=1)

    def second_block(i):
        product = nt(cells, w2_ref[pl.ds(i * 384, 384), :])
        return product[:, :128] + shifted(product[:, 256:]), product[:, 128:256]

    down_first, down_second = second_block(2)
    up_first, up_second = second_block(3)
    halo2s[0, :, :128] = down_first[COLS:]
    halo2s[0, :, 128:] = down_second[COLS:]
    halo2s[1, :, :128] = up_first[:COLS]
    halo2s[1, :, 128:] = up_second[:COLS]
    to_up2 = send(halo2s.at[0], halo2r.at[0], halo_s.at[2], halo_r.at[2], (row_up, m))
    to_down2 = send(halo2s.at[1], halo2r.at[1], halo_s.at[3], halo_r.at[3], (row_down, m))
    to_up2.start()
    to_down2.start()
    even_first, even_second = second_block(0)
    odd_first, odd_second = second_block(1)
    halves = [
        [even_first[:COLS], even_second[:COLS]],
        [odd_first[:COLS] + up_first[COLS:], odd_second[:COLS] + up_second[COLS:]],
        [even_first[COLS:] + down_first[:COLS], even_second[COLS:] + down_second[:COLS]],
        [odd_first[COLS:], odd_second[COLS:]],
    ]
    to_up2.wait_recv()
    to_down2.wait_recv()
    for h in range(2):
        lanes = slice(h * 128, h * 128 + 128)
        halves[0][h] = halves[0][h] + jnp.where(s > 0, halo2r[0, :, lanes], 0.0)
        halves[3][h] = halves[3][h] + jnp.where(s < ROWS - 1, halo2r[1, :, lanes], 0.0)
        for r in range(4):
            block = jnp.maximum(halves[r][h] + b2_ref[...], 0.0)
            two[:, h, r] = block.reshape(PEERS, 8, 128).astype(BF16)
    tiles[m] = two[m]
    twos = exchange(3, lambda peer: two.at[peer], tiles.at[m])
    arrived(twos)
    positions = jnp.concatenate(
        [tiles[j].astype(F32).reshape(64, 128).astype(BF16) for j in range(PEERS)], axis=1
    )
    last = nn(positions, wf_ref[...])
    count = out_ref.shape[-1]
    apart_maps = [(last[:, v * 384 : v * 384 + count] + bf_ref[...]).astype(BF16) for v in range(2)]
    maps = jnp.concatenate(apart_maps, axis=0)
    place = lax.broadcasted_iota(jnp.int32, (128, 128), 0)
    source = (
        ((place >> 1) & 1) * 64
        + ((place ^ (place >> 1)) & 1) * 32
        + (place >> 5) * 8
        + ((place >> 2) & 7)
    )
    order = jnp.where(lax.broadcasted_iota(jnp.int32, (128, 128), 1) == source, 1.0, 0.0).astype(BF16)
    out_ref[...] = nn(order, maps).astype(BF16).reshape(out_ref.shape)

    for p in (1, 2, 3, 4):
        pair[p].wait_send()
    swap.wait_send()

    def sent(t, carry):
        for p in range(4):
            right(t, p).wait_send()
            left(t, p).wait_send()
        return carry

    lax.fori_loop(0, 7, sent, 0)
    for p in range(4):
        right(7, p).wait_send()
    for copy in sums + norms + ones + twos + [to_up, to_down, to_up2, to_down2]:
        copy.wait_send()


def taps_one(weight):
    width = weight.shape[-1]
    blocks = []
    for role in range(2):
        for side in range(2):
            for a in range(2):
                for b in range(2):
                    blocks.append(weight[:, TAPS[role * 2 + a], TAPS[side * 2 + b], :])
                blocks.append(jnp.zeros((32, width), weight.dtype))
    return jnp.concatenate(blocks, axis=0)


def taps_two(weight):
    by_peer = weight.reshape(CHANNELS, 4, 4, PEERS, CHANNELS)
    blank = jnp.zeros((CHANNELS, PEERS, CHANNELS), weight.dtype)
    gap = jnp.zeros((32, PEERS, 2 * CHANNELS), weight.dtype)
    columns = ((1, None), (None, 2), (), (2, 0), (3, 1), (), (None, 3), (0, None), ())
    blocks = []
    for tap in TAPS:
        for pair in columns:
            if pair:
                blocks.append(
                    jnp.concatenate([blank if t is None else by_peer[:, tap, t] for t in pair], axis=2)
                )
            else:
                blocks.append(gap)
    joined = jnp.pad(jnp.concatenate(blocks, axis=0), ((0, 0), (0, 0), (0, 32)))
    return joined.reshape(joined.shape[0], PEERS * 128)


def final_pair(weight):
    by_peer = weight.reshape(PEERS, CHANNELS, -1)
    wide = 384 - by_peer.shape[-1]
    low = jnp.pad(by_peer, ((0, 0), (0, 80), (0, wide)))
    high = jnp.pad(by_peer, ((0, 0), (48, 32), (0, wide)))
    return jnp.concatenate([low, high], axis=2).reshape(PEERS * 128, 768)


def twice(bias):
    return jnp.concatenate([bias, bias, jnp.zeros((32,), bias.dtype)])[None]


def local(
    query, keys, values, resid, out_weight, norm_gain, norm_bias,
    deconv1_weight, deconv1_bias, deconv2_weight, deconv2_bias, final_weight, final_bias,
):
    width = resid.shape[-1]
    count = final_weight.shape[-1]
    operands = (
        query.reshape(COLS, 128),
        keys.reshape(COLS, 128),
        values.reshape(COLS, 128),
        resid.reshape(8, width),
        out_weight,
        norm_gain[None],
        norm_bias[None],
        taps_one(deconv1_weight),
        twice(deconv1_bias),
        taps_two(deconv2_weight),
        twice(deconv2_bias),
        final_pair(final_weight),
        final_bias[None],
    )
    dma = pltpu.SemaphoreType.DMA
    vmem = pltpu.VMEM
    out = pl.pallas_call(
        body,
        out_shape=jax.ShapeDtypeStruct((4, 32, count), BF16),
        in_specs=[pl.BlockSpec(memory_space=pltpu.VMEM)] * len(operands),
        out_specs=pl.BlockSpec(memory_space=pltpu.VMEM),
        scratch_shapes=[
            vmem((ROWS, COLS, 128), BF16),
            vmem((COLS, 128), BF16),
            vmem((2, COLS, 128), BF16),
            vmem((COLS, 128), BF16),
            vmem((COLS, 128), BF16),
            vmem((COLS, 128), BF16),
            vmem((ROWS // CHUNK, 2 * COLS, CHUNK * COLS), F32),
            vmem((PEERS, 8, width), BF16),
            vmem((PEERS, 8, width), BF16),
            vmem((PEERS, 8, width), BF16),
            vmem((2, COLS, 128), F32),
            vmem((2, COLS, 128), F32),
            vmem((PEERS, 2, COLS, 128), BF16),
            vmem((2, COLS, 256), F32),
            vmem((2, COLS, 256), F32),
            vmem((PEERS, 2, 4, 8, 128), BF16),
            vmem((PEERS, 2, 4, 8, 128), BF16),
            dma((5,)),
            dma((5,)),
            dma((8, 4)),
            dma((8, 4)),
            dma((7, 4)),
            dma((7, 4)),
            dma((4, PEERS)),
            dma((4, PEERS)),
            dma((4,)),
            dma((4,)),
        ],
        compiler_params=pltpu.CompilerParams(
            collective_id=0, has_side_effects=True, vmem_limit_bytes=60 * 1024 * 1024
        ),
        name="head",
    )(*operands)
    return out[None]


def solution(mesh):
    placed = (
        P(None, "seq", None, "mp"),
        P(None, "seq", None, "mp"),
        P(None, "seq", None, "mp"),
        P(None, "seq", "mp", None),
        P("mp", None),
        P(),
        P(),
        P("mp", None, None, None),
        P("mp"),
        P("mp", None, None, None),
        P("mp"),
        P(),
        P(),
    )
    return jax.shard_map(
        local, mesh=mesh, in_specs=placed, out_specs=P(None, "seq", "mp", None), check_vma=False
    )
```

```python
import jax
import jax.numpy as jnp
from jax import lax
from jax.experimental import pallas as pl
from jax.experimental.pallas import tpu as pltpu
from jax.sharding import PartitionSpec as P

EPSILON = 1e-06
MESH = pl.DeviceIdType.MESH
F32 = jnp.float32
BF16 = jnp.bfloat16
ROWS = 64
COLS = 64
PEERS = 8
LAYERS = 16
CHANNELS = 48
NONE = -4096
COLUMN_TAPS = (((1, NONE), (NONE, 2)), ((2, 0), (3, 1)), ((NONE, 3), (0, NONE)))


def nt(a, b):
    return lax.dot_general(a, b, (((1,), (1,)), ((), ())), preferred_element_type=F32)


def nn(a, b):
    return lax.dot_general(a, b, (((1,), (0,)), ((), ())), preferred_element_type=F32)


def tn(a, b):
    return lax.dot_general(a, b, (((0,), (0,)), ((), ())), preferred_element_type=F32)


def shifted(field):
    row = lax.broadcasted_iota(jnp.int32, field.shape, 0) & (COLS - 1)
    lane = lax.broadcasted_iota(jnp.int32, field.shape, 1) & 127
    before = jnp.where(row == 0, 0.0, pltpu.roll(field, 1, 0))
    after = jnp.where(row == COLS - 1, 0.0, pltpu.roll(field, field.shape[0] - 1, 0))
    return jnp.where(lane < CHANNELS, before, after)


def body(
    q_ref, k_ref, v_ref, resid_ref, wo_ref, gain_ref, shift_ref, w1_hbm, b1_ref, w2_hbm, b2_ref, wf_hbm, bf_ref,
    out_ref,
    w1_four, w1_raw, w1, w2_four, w2_raw, w2, wf_raw, wf_low, wf_high, low_spread, high_spread, kv, other, qb, qsend, asend, arecv, part, got, normed, halo1s, halo1r, one, halo2s, halo2r, two, tiles,
    pair_s, pair_r, right_s, right_r, left_s, left_r, mp_s, mp_r, halo_s, halo_r, load_s,
):
    s = lax.axis_index("seq")
    m = lax.axis_index("mp")
    core = lax.rem(s, 2)
    y = lax.rem(lax.div(s, 2), 2)
    z = lax.div(s, 4)

    def seq_at(zz, yy, cc):
        return zz * 4 + yy * 2 + cc

    mate = seq_at(z, y, 1 - core)
    across = seq_at(z, 1 - y, core)
    diagonal = seq_at(z, 1 - y, 1 - core)
    z_up = lax.rem(s + 4, ROWS)
    z_down = lax.rem(s + ROWS - 4, ROWS)
    row_up = lax.rem(s + 1, ROWS)
    row_down = lax.rem(s + ROWS - 1, ROWS)

    loads = [
        pltpu.make_async_copy(hbm, raw, load_s.at[i])
        for i, (hbm, raw) in enumerate(((w1_hbm, w1_four), (w2_hbm, w2_four), (wf_hbm, wf_raw)))
    ]
    for copy in loads:
        copy.start()

    barrier = pltpu.get_barrier_semaphore()
    greeted = [(mate, m), (across, m), (diagonal, m), (z_up, m), (z_down, m), (row_up, m), (row_down, m)]
    greeted += [(s, lax.rem(m + d, PEERS)) for d in range(1, PEERS)]
    for device in greeted:
        pl.semaphore_signal(barrier, inc=1, device_id=device, device_id_type=MESH)

    lane = lax.broadcasted_iota(jnp.int32, (COLS, 128), 1)
    low = lane < 64
    k = k_ref[...].astype(F32)
    v = v_ref[...].astype(F32)
    q = q_ref[...].astype(F32) * 0.125
    first = jnp.where(low, k, pltpu.roll(v, 64, 1))
    second = jnp.where(low, pltpu.roll(k, 64, 1), v)
    q_first = jnp.where(low, q, 0.0)
    q_second = jnp.where(low, pltpu.roll(q, 64, 1), 0.0)
    is_first = core == 0
    kv[s] = jnp.where(is_first, first, second).astype(BF16)
    other[...] = jnp.where(is_first, second, first).astype(BF16)
    qb[core] = jnp.where(is_first, q_first, q_second).astype(BF16)
    qsend[...] = jnp.where(is_first, q_second, q_first).astype(BF16)

    pl.semaphore_wait(barrier, len(greeted))

    def send(src, dst, ssem, rsem, device):
        return pltpu.make_async_remote_copy(
            src_ref=src, dst_ref=dst, send_sem=ssem, recv_sem=rsem, device_id=device, device_id_type=MESH
        )

    def piece(layer, p):
        yy = y if p < 2 else 1 - y
        cc = core if p % 2 == 0 else 1 - core
        return seq_at(layer, yy, cc)

    def right(t, p):
        block = kv.at[piece(lax.rem(z - t + LAYERS, LAYERS), p)]
        return send(block, block, right_s.at[t, p], right_r.at[t, p], (z_up, m))

    def left(t, p):
        block = kv.at[piece(lax.rem(z + t, LAYERS), p)]
        return send(block, block, left_s.at[t, p], left_r.at[t, p], (z_down, m))

    right(0, 0).start()
    left(0, 0).start()
    pair = [
        None,
        send(other, kv.at[s], pair_s.at[1], pair_r.at[1], (mate, m)),
        send(kv.at[s], kv.at[s], pair_s.at[2], pair_r.at[2], (across, m)),
        send(other, kv.at[s], pair_s.at[3], pair_r.at[3], (diagonal, m)),
        send(qsend, qb.at[core], pair_s.at[0], pair_r.at[0], (mate, m)),
    ]
    for p in (1, 2, 3, 4):
        pair[p].start()
    for p in (1, 2, 3):
        pair[p].wait_recv()
        right(0, p).start()
        left(0, p).start()
    pair[4].wait_recv()

    def attend(state, layers):
        top, total, mixed = state
        block = jnp.concatenate([kv[pl.ds(layer * 4, 4)].reshape(4 * COLS, 128) for layer in layers], axis=0)
        fresh = nt(qb[...].reshape(2 * COLS, 128), block)
        best = jnp.maximum(top, jnp.max(fresh, axis=1, keepdims=True))
        fade = jnp.exp(top - best)
        exps = jnp.exp(fresh - best)
        return (
            best,
            total * fade + jnp.sum(exps, axis=1, keepdims=True),
            mixed * fade + nn(exps.astype(BF16), block),
        )

    def arrange_one(i):
        row_tap = lax.rem(lax.div(i, 4) * 2 + lax.rem(i, 2) + 1, 4)
        side = lax.rem(lax.div(i, 2), 2) * 2
        col_tap = jnp.where(group, lax.rem(side + 2, 4), lax.rem(side + 1, 4))
        source = channel * 16 + row_tap * 4 + col_tap
        w1[pl.ds(pl.multiple_of(i * 128, 128), 128), :] = nn(pick(source, 768), w1_raw[...]).astype(BF16)

    def arrange_two(i, n):
        row_tap = lax.rem(i + 1, 4)
        for b, spread in ((0, low_spread), (1, high_spread)):
            first_tap, second_tap = [
                jnp.where(n == 0, COLUMN_TAPS[0][g][b], jnp.where(n == 1, COLUMN_TAPS[1][g][b], COLUMN_TAPS[2][g][b]))
                for g in range(2)
            ]
            col_tap = jnp.where(group, second_tap, first_tap)
            rows = nn(pick(channel * 16 + row_tap * 4 + col_tap, 768), w2_raw[...]).astype(BF16)
            placed = nn(rows, spread[...])
            full = placed if b == 0 else full + placed
        w2[pl.ds(pl.multiple_of(i * 384 + n * 128, 128), 128), :] = full.astype(BF16)

    line = lax.broadcasted_iota(jnp.int32, (128, 768), 0)
    group = line >= CHANNELS
    channel = jnp.where(group, line - CHANNELS, line)
    kept = line < 2 * CHANNELS

    def pick(source, width):
        wanted = jnp.where(kept, source, -1)
        return jnp.where(lax.broadcasted_iota(jnp.int32, (128, width), 1) == wanted, 1.0, 0.0).astype(BF16)

    wide = lax.broadcasted_iota(jnp.int32, (PEERS * CHANNELS, PEERS * 128), 1)
    narrow = lax.broadcasted_iota(jnp.int32, (PEERS * CHANNELS, PEERS * 128), 0)
    within = wide & 127
    home = (wide >> 7) * CHANNELS + within
    low_spread[...] = jnp.where((narrow == home) & (within < CHANNELS), 1.0, 0.0).astype(BF16)
    high_spread[...] = jnp.where(
        (narrow == home - CHANNELS) & (within >= CHANNELS) & (within < 2 * CHANNELS), 1.0, 0.0
    ).astype(BF16)
    bias1 = twice(b1_ref[...])
    bias2 = twice(b2_ref[...])
    for copy in loads:
        copy.wait()

    def flatten(four, raw, first, last):
        def rows_of(e, carry):
            rows = pl.ds(pl.multiple_of(e * 32, 32), 32)
            raw[rows, :] = four[pl.ds(e * 2, 2)].astype(F32).reshape(32, raw.shape[1]).astype(BF16)
            return carry

        lax.fori_loop(first, last, rows_of, 0)

    def arrange_part(first):
        def chunk(i, carry):
            arrange_two(lax.div(i, 3), lax.rem(i, 3))
            return carry

        lax.fori_loop(first, first + 4, chunk, 0)

    start = (
        jnp.full((2 * COLS, 1), -jnp.inf, F32),
        jnp.zeros((2 * COLS, 1), F32),
        jnp.zeros((2 * COLS, 128), F32),
    )
    state = attend(start, [z])

    def ring(t, state):
        for p in range(4):
            right(t - 1, p).wait_recv()
            right(t, p).start()
            left(t - 1, p).wait_recv()
            left(t, p).start()
        return attend(state, [lax.rem(z - t + LAYERS, LAYERS), lax.rem(z + t, LAYERS)])

    def ring_flatten(t, state):
        state = ring(t, state)
        flatten(w1_four, w1_raw, (t - 1) * 8, t * 8)
        return state

    def ring_arrange(t, state):
        state = ring(t, state)
        arrange_one((t - 4) * 2)
        arrange_one((t - 4) * 2 + 1)
        return state

    state = lax.fori_loop(1, 4, ring_flatten, state)
    state = lax.fori_loop(4, 7, ring_arrange, state)
    for p in range(4):
        right(6, p).wait_recv()
        right(7, p).start()
    for p in range(4):
        left(6, p).wait_recv()
    state = attend(state, [lax.rem(z + 9, LAYERS), lax.rem(z + 7, LAYERS)])
    arrange_one(6)
    arrange_one(7)
    for p in range(4):
        right(7, p).wait_recv()
    top, total, mixed = attend(state, [lax.rem(z + 8, LAYERS)])
    attended = mixed / total
    placed = jnp.where(is_first, jnp.where(low, pltpu.roll(attended[:COLS], 64, 1), 0.0), jnp.where(low, 0.0, attended[:COLS]))
    placed_too = jnp.where(is_first, jnp.where(low, pltpu.roll(attended[COLS:], 64, 1), 0.0), jnp.where(low, 0.0, attended[COLS:]))
    asend[...] = jnp.where(is_first, placed_too, placed).astype(BF16)
    swap = send(asend, arecv, pair_s.at[4], pair_r.at[4], (mate, m))
    swap.start()
    mine = jnp.where(is_first, placed, placed_too).astype(BF16)
    swap.wait_recv()
    rows = (mine.astype(F32) + arecv[...].astype(F32)).astype(BF16)

    def exchange(phase, source, target):
        copies = []
        for d in range(1, PEERS):
            peer = lax.rem(m + d, PEERS)
            copies.append(send(source(peer), target, mp_s.at[phase, d], mp_r.at[phase, d], (s, peer)))
        for copy in copies:
            copy.start()
        return copies

    def arrived(copies):
        for copy in copies:
            copy.wait_recv()

    part[...] = nn(rows, wo_ref[...]).reshape(PEERS, 8, -1).astype(BF16)
    sums = exchange(0, lambda peer: part.at[peer], got.at[m])
    stream = resid_ref[...].astype(F32) + part[m].astype(F32)
    got[m] = jnp.zeros(got.shape[1:], BF16)
    flatten(w2_four, w2_raw, 0, CHANNELS // 2)
    arrange_part(0)
    arrived(sums)
    for j in range(PEERS):
        stream = stream + got[j].astype(F32)
    center = jnp.mean(stream, axis=1, keepdims=True)
    apart = stream - center
    variance = jnp.mean(apart * apart, axis=1, keepdims=True)
    normed[m] = (apart * lax.rsqrt(variance + EPSILON) * gain_ref[...][None] + shift_ref[...][None]).astype(BF16)
    norms = exchange(1, lambda peer: normed.at[m], normed.at[m])
    arrange_part(4)
    arrived(norms)
    tokens = normed[...].astype(F32).reshape(COLS, -1).astype(BF16)

    def first_block(i):
        return nt(tokens, w1[pl.ds(i * 256, 256), :])

    crossing = first_block(2) + shifted(first_block(3))
    halo1s[0] = crossing[:, :128]
    halo1s[1] = crossing[:, 128:]
    to_up = send(halo1s.at[0], halo1r.at[0], halo_s.at[0], halo_r.at[0], (row_up, m))
    to_down = send(halo1s.at[1], halo1r.at[1], halo_s.at[1], halo_r.at[1], (row_down, m))
    to_up.start()
    to_down.start()
    inside = first_block(0) + shifted(first_block(1))
    to_up.wait_recv()
    to_down.wait_recv()
    upper = inside[:, :128] + jnp.where(s > 0, halo1r[0], 0.0)
    lower = inside[:, 128:] + jnp.where(s < ROWS - 1, halo1r[1], 0.0)
    one[m, 0] = jnp.maximum(upper + bias1, 0.0).astype(BF16)
    one[m, 1] = jnp.maximum(lower + bias1, 0.0).astype(BF16)
    ones = exchange(2, lambda peer: one.at[m], one.at[m])
    arrange_part(8)
    wf_low[...] = nn(wf_raw[...], low_spread[...]).astype(BF16)
    wf_high[...] = nn(wf_raw[...], high_spread[...]).astype(BF16)
    arrived(ones)
    cells = jnp.concatenate([one[j].reshape(2 * COLS, 128) for j in range(PEERS)], axis=1)

    def second_block(i):
        product = nt(cells, w2[pl.ds(i * 384, 384), :])
        return product[:, :128] + shifted(product[:, 256:]), product[:, 128:256]

    down_first, down_second = second_block(2)
    up_first, up_second = second_block(3)
    halo2s[0, :, :128] = down_first[COLS:]
    halo2s[0, :, 128:] = down_second[COLS:]
    halo2s[1, :, :128] = up_first[:COLS]
    halo2s[1, :, 128:] = up_second[:COLS]
    to_up2 = send(halo2s.at[0], halo2r.at[0], halo_s.at[2], halo_r.at[2], (row_up, m))
    to_down2 = send(halo2s.at[1], halo2r.at[1], halo_s.at[3], halo_r.at[3], (row_down, m))
    to_up2.start()
    to_down2.start()
    even_first, even_second = second_block(0)
    odd_first, odd_second = second_block(1)
    halves = [
        [even_first[:COLS], even_second[:COLS]],
        [odd_first[:COLS] + up_first[COLS:], odd_second[:COLS] + up_second[COLS:]],
        [even_first[COLS:] + down_first[:COLS], even_second[COLS:] + down_second[:COLS]],
        [odd_first[COLS:], odd_second[COLS:]],
    ]
    to_up2.wait_recv()
    to_down2.wait_recv()
    for h in range(2):
        lanes = slice(h * 128, h * 128 + 128)
        halves[0][h] = halves[0][h] + jnp.where(s > 0, halo2r[0, :, lanes], 0.0)
        halves[3][h] = halves[3][h] + jnp.where(s < ROWS - 1, halo2r[1, :, lanes], 0.0)
        for r in range(4):
            block = jnp.maximum(halves[r][h] + bias2, 0.0)
            two[:, h, r] = block.reshape(PEERS, 8, 128).astype(BF16)
    tiles[m] = two[m]
    twos = exchange(3, lambda peer: two.at[peer], tiles.at[m])
    arrived(twos)
    positions = jnp.concatenate(
        [tiles[j].astype(F32).reshape(64, 128).astype(BF16) for j in range(PEERS)], axis=1
    )
    apart_maps = [(nt(positions, weight[...]) + bf_ref[...][None]).astype(BF16) for weight in (wf_low, wf_high)]
    maps = jnp.concatenate(apart_maps, axis=0)
    place = lax.broadcasted_iota(jnp.int32, (128, 128), 0)
    source = (
        ((place >> 1) & 1) * 64
        + ((place ^ (place >> 1)) & 1) * 32
        + (place >> 5) * 8
        + ((place >> 2) & 7)
    )
    order = jnp.where(lax.broadcasted_iota(jnp.int32, (128, 128), 1) == source, 1.0, 0.0).astype(BF16)
    out_ref[...] = nn(order, maps).astype(BF16).reshape(out_ref.shape)

    for p in (1, 2, 3, 4):
        pair[p].wait_send()
    swap.wait_send()

    def sent(t, carry):
        for p in range(4):
            right(t, p).wait_send()
            left(t, p).wait_send()
        return carry

    lax.fori_loop(0, 7, sent, 0)
    for p in range(4):
        right(7, p).wait_send()
    for copy in sums + norms + ones + twos + [to_up, to_down, to_up2, to_down2]:
        copy.wait_send()


def twice(bias):
    lane = lax.broadcasted_iota(jnp.int32, (CHANNELS, 128), 1)
    home = jnp.where(lane < CHANNELS, lane, lane - CHANNELS)
    spread = jnp.where(lax.broadcasted_iota(jnp.int32, (CHANNELS, 128), 0) == home, 1.0, 0.0)
    return jnp.dot(jnp.broadcast_to(bias[None], (8, CHANNELS)), spread, precision=lax.Precision.HIGHEST)[:1]


def local(
    query, keys, values, resid, out_weight, norm_gain, norm_bias,
    deconv1_weight, deconv1_bias, deconv2_weight, deconv2_bias, final_weight, final_bias,
):
    width = resid.shape[-1]
    count = final_weight.shape[-1]
    operands = (
        query.reshape(COLS, 128),
        keys.reshape(COLS, 128),
        values.reshape(COLS, 128),
        resid.reshape(8, width),
        out_weight,
        norm_gain,
        norm_bias,
        deconv1_weight,
        deconv1_bias,
        deconv2_weight,
        deconv2_bias,
        final_weight.T,
        final_bias,
    )
    dma = pltpu.SemaphoreType.DMA
    vmem = pltpu.VMEM
    out = pl.pallas_call(
        body,
        out_shape=jax.ShapeDtypeStruct((4, 32, count), BF16),
        in_specs=[
            pl.BlockSpec(memory_space=pl.ANY if i in (7, 9, 11) else pltpu.VMEM) for i in range(len(operands))
        ],
        out_specs=pl.BlockSpec(memory_space=pltpu.VMEM),
        scratch_shapes=[
            vmem((CHANNELS, 4, 4, width), BF16),
            vmem((768, width), BF16),
            vmem((1024, width), BF16),
            vmem((CHANNELS, 4, 4, 384), BF16),
            vmem((768, 384), BF16),
            vmem((1536, 1024), BF16),
            vmem((count, 384), BF16),
            vmem((count, 1024), BF16),
            vmem((count, 1024), BF16),
            vmem((384, 1024), BF16),
            vmem((384, 1024), BF16),
            vmem((ROWS, COLS, 128), BF16),
            vmem((COLS, 128), BF16),
            vmem((2, COLS, 128), BF16),
            vmem((COLS, 128), BF16),
            vmem((COLS, 128), BF16),
            vmem((COLS, 128), BF16),
            vmem((PEERS, 8, width), BF16),
            vmem((PEERS, 8, width), BF16),
            vmem((PEERS, 8, width), BF16),
            vmem((2, COLS, 128), F32),
            vmem((2, COLS, 128), F32),
            vmem((PEERS, 2, COLS, 128), BF16),
            vmem((2, COLS, 256), F32),
            vmem((2, COLS, 256), F32),
            vmem((PEERS, 2, 4, 8, 128), BF16),
            vmem((PEERS, 2, 4, 8, 128), BF16),
            dma((5,)),
            dma((5,)),
            dma((8, 4)),
            dma((8, 4)),
            dma((7, 4)),
            dma((7, 4)),
            dma((4, PEERS)),
            dma((4, PEERS)),
            dma((4,)),
            dma((4,)),
            dma((3,)),
        ],
        compiler_params=pltpu.CompilerParams(
            collective_id=0, has_side_effects=True, vmem_limit_bytes=60 * 1024 * 1024
        ),
        name="head",
    )(*operands)
    return out[None]


def solution(mesh):
    placed = (
        P(None, "seq", None, "mp"),
        P(None, "seq", None, "mp"),
        P(None, "seq", None, "mp"),
        P(None, "seq", "mp", None),
        P("mp", None),
        P(),
        P(),
        P("mp", None, None, None),
        P("mp"),
        P("mp", None, None, None),
        P("mp"),
        P(),
        P(),
    )
    return jax.shard_map(
        local, mesh=mesh, in_specs=placed, out_specs=P(None, "seq", "mp", None), check_vma=False
    )
```

```python
import jax
import jax.numpy as jnp
from jax import lax
from jax.experimental import pallas as pl
from jax.experimental.pallas import tpu as pltpu
from jax.sharding import PartitionSpec as P

EPSILON = 1e-06
MESH = pl.DeviceIdType.MESH
F32 = jnp.float32
BF16 = jnp.bfloat16
ROWS = 64
COLS = 64
PEERS = 8
LAYERS = 16
CHANNELS = 48
TAPS = (1, 2, 3, 0)
COLUMN_TAPS = (((1, None), (None, 2)), ((2, 0), (3, 1)), ((None, 3), (0, None)))


def nt(a, b):
    return lax.dot_general(a, b, (((1,), (1,)), ((), ())), preferred_element_type=F32)


def nn(a, b):
    return lax.dot_general(a, b, (((1,), (0,)), ((), ())), preferred_element_type=F32)


def tn(a, b):
    return lax.dot_general(a, b, (((0,), (0,)), ((), ())), preferred_element_type=F32)


def shifted(field):
    row = lax.broadcasted_iota(jnp.int32, field.shape, 0) & (COLS - 1)
    lane = lax.broadcasted_iota(jnp.int32, field.shape, 1) & 127
    before = jnp.where(row == 0, 0.0, pltpu.roll(field, 1, 0))
    after = jnp.where(row == COLS - 1, 0.0, pltpu.roll(field, field.shape[0] - 1, 0))
    return jnp.where(lane < CHANNELS, before, after)


def body(
    q_ref, k_ref, v_ref, resid_ref, wo_ref, gain_ref, shift_ref, w1_hbm, b1_ref, w2_hbm, b2_ref, wf_hbm, bf_ref,
    out_ref,
    w1_four, w1_raw, w1, w2_four, w2_raw, w2_tap, w2_low, w2_high, w2, wf_raw, wf_low, wf_high, low_spread, high_spread, kv, other, qb, qsend, asend, arecv, part, got, normed, halo1s, halo1r, one, halo2s, halo2r, two, tiles,
    pair_s, pair_r, right_s, right_r, left_s, left_r, mp_s, mp_r, halo_s, halo_r, load_s,
):
    s = lax.axis_index("seq")
    m = lax.axis_index("mp")
    core = lax.rem(s, 2)
    y = lax.rem(lax.div(s, 2), 2)
    z = lax.div(s, 4)

    def seq_at(zz, yy, cc):
        return zz * 4 + yy * 2 + cc

    mate = seq_at(z, y, 1 - core)
    across = seq_at(z, 1 - y, core)
    diagonal = seq_at(z, 1 - y, 1 - core)
    z_up = lax.rem(s + 4, ROWS)
    z_down = lax.rem(s + ROWS - 4, ROWS)
    row_up = lax.rem(s + 1, ROWS)
    row_down = lax.rem(s + ROWS - 1, ROWS)

    loads = [
        pltpu.make_async_copy(hbm, raw, load_s.at[i])
        for i, (hbm, raw) in enumerate(((w1_hbm, w1_four), (w2_hbm, w2_four), (wf_hbm, wf_raw)))
    ]
    for copy in loads:
        copy.start()

    barrier = pltpu.get_barrier_semaphore()
    greeted = [(mate, m), (across, m), (diagonal, m), (z_up, m), (z_down, m), (row_up, m), (row_down, m)]
    greeted += [(s, lax.rem(m + d, PEERS)) for d in range(1, PEERS)]
    for device in greeted:
        pl.semaphore_signal(barrier, inc=1, device_id=device, device_id_type=MESH)

    lane = lax.broadcasted_iota(jnp.int32, (COLS, 128), 1)
    low = lane < 64
    k = k_ref[...].astype(F32)
    v = v_ref[...].astype(F32)
    q = q_ref[...].astype(F32) * 0.125
    first = jnp.where(low, k, pltpu.roll(v, 64, 1))
    second = jnp.where(low, pltpu.roll(k, 64, 1), v)
    q_first = jnp.where(low, q, 0.0)
    q_second = jnp.where(low, pltpu.roll(q, 64, 1), 0.0)
    is_first = core == 0
    kv[s] = jnp.where(is_first, first, second).astype(BF16)
    other[...] = jnp.where(is_first, second, first).astype(BF16)
    qb[core] = jnp.where(is_first, q_first, q_second).astype(BF16)
    qsend[...] = jnp.where(is_first, q_second, q_first).astype(BF16)

    pl.semaphore_wait(barrier, len(greeted))

    def send(src, dst, ssem, rsem, device):
        return pltpu.make_async_remote_copy(
            src_ref=src, dst_ref=dst, send_sem=ssem, recv_sem=rsem, device_id=device, device_id_type=MESH
        )

    def piece(layer, p):
        yy = y if p < 2 else 1 - y
        cc = core if p % 2 == 0 else 1 - core
        return seq_at(layer, yy, cc)

    def right(t, p):
        block = kv.at[piece(lax.rem(z - t + LAYERS, LAYERS), p)]
        return send(block, block, right_s.at[t, p], right_r.at[t, p], (z_up, m))

    def left(t, p):
        block = kv.at[piece(lax.rem(z + t, LAYERS), p)]
        return send(block, block, left_s.at[t, p], left_r.at[t, p], (z_down, m))

    right(0, 0).start()
    left(0, 0).start()
    pair = [
        None,
        send(other, kv.at[s], pair_s.at[1], pair_r.at[1], (mate, m)),
        send(kv.at[s], kv.at[s], pair_s.at[2], pair_r.at[2], (across, m)),
        send(other, kv.at[s], pair_s.at[3], pair_r.at[3], (diagonal, m)),
        send(qsend, qb.at[core], pair_s.at[0], pair_r.at[0], (mate, m)),
    ]
    for p in (1, 2, 3, 4):
        pair[p].start()
    for p in (1, 2, 3):
        pair[p].wait_recv()
        right(0, p).start()
        left(0, p).start()
    pair[4].wait_recv()

    def attend(state, layers):
        top, total, mixed = state
        block = jnp.concatenate([kv[pl.ds(layer * 4, 4)].reshape(4 * COLS, 128) for layer in layers], axis=0)
        fresh = nt(qb[...].reshape(2 * COLS, 128), block)
        best = jnp.maximum(top, jnp.max(fresh, axis=1, keepdims=True))
        fade = jnp.exp(top - best)
        exps = jnp.exp(fresh - best)
        return (
            best,
            total * fade + jnp.sum(exps, axis=1, keepdims=True),
            mixed * fade + nn(exps.astype(BF16), block),
        )

    def arrange_one(i):
        row_tap = lax.rem(lax.div(i, 4) * 2 + lax.rem(i, 2) + 1, 4)
        side = lax.rem(lax.div(i, 2), 2) * 2
        for b in range(2):
            tap = row_tap * 4 + lax.rem(side + b + 1, 4)
            rows = pl.ds(pl.multiple_of(i * 128 + b * CHANNELS, 16), CHANNELS)
            for c in range(w1_raw.shape[0]):
                lanes = slice(c * 128, c * 128 + 128)
                w1[rows, lanes] = w1_raw[c, pl.ds(tap, CHANNELS, stride=16), :].astype(BF16)

    wide = lax.broadcasted_iota(jnp.int32, (PEERS * CHANNELS, PEERS * 128), 1)
    narrow = lax.broadcasted_iota(jnp.int32, (PEERS * CHANNELS, PEERS * 128), 0)
    within = wide & 127
    home = (wide >> 7) * CHANNELS + within
    low_spread[...] = jnp.where((narrow == home) & (within < CHANNELS), 1.0, 0.0).astype(BF16)
    high_spread[...] = jnp.where(
        (narrow == home - CHANNELS) & (within >= CHANNELS) & (within < 2 * CHANNELS), 1.0, 0.0
    ).astype(BF16)
    bias1 = twice(b1_ref[...])
    bias2 = twice(b2_ref[...])
    for copy in loads:
        copy.wait()

    def flatten(four, raw, first, last):
        def rows_of(e, carry):
            rows = pl.ds(pl.multiple_of(e * 32, 32), 32)
            flat = four[pl.ds(e * 2, 2)].astype(F32).reshape(32, four.shape[-1])
            for c in range(raw.shape[0]):
                raw[c, rows, :] = flat[:, c * 128 : c * 128 + 128]
            return carry

        lax.fori_loop(first, last, rows_of, 0)

    start = (
        jnp.full((2 * COLS, 1), -jnp.inf, F32),
        jnp.zeros((2 * COLS, 1), F32),
        jnp.zeros((2 * COLS, 128), F32),
    )
    state = attend(start, [z])
    for i in range(8):
        w1[i * 128 + 2 * CHANNELS : i * 128 + 128, :] = jnp.zeros((32, w1.shape[1]), BF16)
    for i in range(12):
        w2[i * 128 + 2 * CHANNELS : i * 128 + 128, :] = jnp.zeros((32, w2.shape[1]), BF16)

    def ring(t, state):
        for p in range(4):
            right(t - 1, p).wait_recv()
            right(t, p).start()
            left(t - 1, p).wait_recv()
            left(t, p).start()
        return attend(state, [lax.rem(z - t + LAYERS, LAYERS), lax.rem(z + t, LAYERS)])

    def ring_flatten(t, state):
        state = ring(t, state)
        flatten(w1_four, w1_raw, (t - 1) * 8, t * 8)
        return state

    def ring_arrange(t, state):
        state = ring(t, state)
        arrange_one((t - 4) * 2)
        arrange_one((t - 4) * 2 + 1)
        return state

    state = lax.fori_loop(1, 4, ring_flatten, state)
    state = lax.fori_loop(4, 7, ring_arrange, state)
    for p in range(4):
        right(6, p).wait_recv()
        right(7, p).start()
    for p in range(4):
        left(6, p).wait_recv()
    state = attend(state, [lax.rem(z + 9, LAYERS), lax.rem(z + 7, LAYERS)])
    arrange_one(6)
    arrange_one(7)
    for p in range(4):
        right(7, p).wait_recv()
    top, total, mixed = attend(state, [lax.rem(z + 8, LAYERS)])
    attended = mixed / total
    placed = jnp.where(is_first, jnp.where(low, pltpu.roll(attended[:COLS], 64, 1), 0.0), jnp.where(low, 0.0, attended[:COLS]))
    placed_too = jnp.where(is_first, jnp.where(low, pltpu.roll(attended[COLS:], 64, 1), 0.0), jnp.where(low, 0.0, attended[COLS:]))
    asend[...] = jnp.where(is_first, placed_too, placed).astype(BF16)
    swap = send(asend, arecv, pair_s.at[4], pair_r.at[4], (mate, m))
    swap.start()
    mine = jnp.where(is_first, placed, placed_too).astype(BF16)
    swap.wait_recv()
    rows = (mine.astype(F32) + arecv[...].astype(F32)).astype(BF16)

    def exchange(phase, source, target):
        copies = []
        for d in range(1, PEERS):
            peer = lax.rem(m + d, PEERS)
            copies.append(send(source(peer), target, mp_s.at[phase, d], mp_r.at[phase, d], (s, peer)))
        for copy in copies:
            copy.start()
        return copies

    def arrived(copies):
        for copy in copies:
            copy.wait_recv()

    part[...] = nn(rows, wo_ref[...]).reshape(PEERS, 8, -1).astype(BF16)
    sums = exchange(0, lambda peer: part.at[peer], got.at[m])
    stream = resid_ref[...].astype(F32) + part[m].astype(F32)
    got[m] = jnp.zeros(got.shape[1:], BF16)
    flatten(w2_four, w2_raw, 0, CHANNELS // 2)
    for tap in range(16):
        for c in range(w2_raw.shape[0]):
            rows = w2_raw[c, pl.ds(tap, CHANNELS, stride=16), :]
            w2_tap[tap * CHANNELS : (tap + 1) * CHANNELS, c * 128 : c * 128 + 128] = rows.astype(BF16)
    arrived(sums)
    for j in range(PEERS):
        stream = stream + got[j].astype(F32)
    center = jnp.mean(stream, axis=1, keepdims=True)
    apart = stream - center
    variance = jnp.mean(apart * apart, axis=1, keepdims=True)
    normed[m] = (apart * lax.rsqrt(variance + EPSILON) * gain_ref[...][None] + shift_ref[...][None]).astype(BF16)
    norms = exchange(1, lambda peer: normed.at[m], normed.at[m])
    w2_low[...] = nn(w2_tap[...], low_spread[...]).astype(BF16)
    w2_high[...] = nn(w2_tap[...], high_spread[...]).astype(BF16)
    arrived(norms)
    tokens = normed[...].astype(F32).reshape(COLS, -1).astype(BF16)

    def first_block(i):
        return nt(tokens, w1[pl.ds(i * 256, 256), :])

    crossing = first_block(2) + shifted(first_block(3))
    halo1s[0] = crossing[:, :128]
    halo1s[1] = crossing[:, 128:]
    to_up = send(halo1s.at[0], halo1r.at[0], halo_s.at[0], halo_r.at[0], (row_up, m))
    to_down = send(halo1s.at[1], halo1r.at[1], halo_s.at[1], halo_r.at[1], (row_down, m))
    to_up.start()
    to_down.start()
    inside = first_block(0) + shifted(first_block(1))
    to_up.wait_recv()
    to_down.wait_recv()
    upper = inside[:, :128] + jnp.where(s > 0, halo1r[0], 0.0)
    lower = inside[:, 128:] + jnp.where(s < ROWS - 1, halo1r[1], 0.0)
    one[m, 0] = jnp.maximum(upper + bias1, 0.0).astype(BF16)
    one[m, 1] = jnp.maximum(lower + bias1, 0.0).astype(BF16)
    ones = exchange(2, lambda peer: one.at[m], one.at[m])
    for i in range(4):
        for n in range(3):
            base = i * 384 + n * 128
            for g in range(2):
                blocks = [
                    spread[(TAPS[i] * 4 + t) * CHANNELS : (TAPS[i] * 4 + t + 1) * CHANNELS, :]
                    for spread, t in zip((w2_low, w2_high), COLUMN_TAPS[n][g])
                    if t is not None
                ]
                w2[base + g * CHANNELS : base + (g + 1) * CHANNELS, :] = sum(blocks[1:], blocks[0])
    wf_low[...] = nn(wf_raw[...], low_spread[...]).astype(BF16)
    wf_high[...] = nn(wf_raw[...], high_spread[...]).astype(BF16)
    arrived(ones)
    cells = jnp.concatenate([one[j].reshape(2 * COLS, 128) for j in range(PEERS)], axis=1)

    def second_block(i):
        product = nt(cells, w2[pl.ds(i * 384, 384), :])
        return product[:, :128] + shifted(product[:, 256:]), product[:, 128:256]

    down_first, down_second = second_block(2)
    up_first, up_second = second_block(3)
    halo2s[0, :, :128] = down_first[COLS:]
    halo2s[0, :, 128:] = down_second[COLS:]
    halo2s[1, :, :128] = up_first[:COLS]
    halo2s[1, :, 128:] = up_second[:COLS]
    to_up2 = send(halo2s.at[0], halo2r.at[0], halo_s.at[2], halo_r.at[2], (row_up, m))
    to_down2 = send(halo2s.at[1], halo2r.at[1], halo_s.at[3], halo_r.at[3], (row_down, m))
    to_up2.start()
    to_down2.start()
    even_first, even_second = second_block(0)
    odd_first, odd_second = second_block(1)
    halves = [
        [even_first[:COLS], even_second[:COLS]],
        [odd_first[:COLS] + up_first[COLS:], odd_second[:COLS] + up_second[COLS:]],
        [even_first[COLS:] + down_first[:COLS], even_second[COLS:] + down_second[:COLS]],
        [odd_first[COLS:], odd_second[COLS:]],
    ]
    to_up2.wait_recv()
    to_down2.wait_recv()
    for h in range(2):
        lanes = slice(h * 128, h * 128 + 128)
        halves[0][h] = halves[0][h] + jnp.where(s > 0, halo2r[0, :, lanes], 0.0)
        halves[3][h] = halves[3][h] + jnp.where(s < ROWS - 1, halo2r[1, :, lanes], 0.0)
        for r in range(4):
            block = jnp.maximum(halves[r][h] + bias2, 0.0)
            two[:, h, r] = block.reshape(PEERS, 8, 128).astype(BF16)
    tiles[m] = two[m]
    twos = exchange(3, lambda peer: two.at[peer], tiles.at[m])
    arrived(twos)
    positions = jnp.concatenate(
        [tiles[j].astype(F32).reshape(64, 128).astype(BF16) for j in range(PEERS)], axis=1
    )
    apart_maps = [(nt(positions, weight[...]) + bf_ref[...][None]).astype(BF16) for weight in (wf_low, wf_high)]
    maps = jnp.concatenate(apart_maps, axis=0)
    place = lax.broadcasted_iota(jnp.int32, (128, 128), 0)
    source = (
        ((place >> 1) & 1) * 64
        + ((place ^ (place >> 1)) & 1) * 32
        + (place >> 5) * 8
        + ((place >> 2) & 7)
    )
    order = jnp.where(lax.broadcasted_iota(jnp.int32, (128, 128), 1) == source, 1.0, 0.0).astype(BF16)
    out_ref[...] = nn(order, maps).astype(BF16).reshape(out_ref.shape)

    for p in (1, 2, 3, 4):
        pair[p].wait_send()
    swap.wait_send()

    def sent(t, carry):
        for p in range(4):
            right(t, p).wait_send()
            left(t, p).wait_send()
        return carry

    lax.fori_loop(0, 7, sent, 0)
    for p in range(4):
        right(7, p).wait_send()
    for copy in sums + norms + ones + twos + [to_up, to_down, to_up2, to_down2]:
        copy.wait_send()


def twice(bias):
    lane = lax.broadcasted_iota(jnp.int32, (CHANNELS, 128), 1)
    home = jnp.where(lane < CHANNELS, lane, lane - CHANNELS)
    spread = jnp.where(lax.broadcasted_iota(jnp.int32, (CHANNELS, 128), 0) == home, 1.0, 0.0)
    return jnp.dot(jnp.broadcast_to(bias[None], (8, CHANNELS)), spread, precision=lax.Precision.HIGHEST)[:1]


def local(
    query, keys, values, resid, out_weight, norm_gain, norm_bias,
    deconv1_weight, deconv1_bias, deconv2_weight, deconv2_bias, final_weight, final_bias,
):
    width = resid.shape[-1]
    count = final_weight.shape[-1]
    operands = (
        query.reshape(COLS, 128),
        keys.reshape(COLS, 128),
        values.reshape(COLS, 128),
        resid.reshape(8, width),
        out_weight,
        norm_gain,
        norm_bias,
        deconv1_weight,
        deconv1_bias,
        deconv2_weight,
        deconv2_bias,
        final_weight.T,
        final_bias,
    )
    dma = pltpu.SemaphoreType.DMA
    vmem = pltpu.VMEM
    out = pl.pallas_call(
        body,
        out_shape=jax.ShapeDtypeStruct((4, 32, count), BF16),
        in_specs=[
            pl.BlockSpec(memory_space=pl.ANY if i in (7, 9, 11) else pltpu.VMEM) for i in range(len(operands))
        ],
        out_specs=pl.BlockSpec(memory_space=pltpu.VMEM),
        scratch_shapes=[
            vmem((CHANNELS, 4, 4, width), BF16),
            vmem((width // 128, 768, 128), F32),
            vmem((1024, width), BF16),
            vmem((CHANNELS, 4, 4, 384), BF16),
            vmem((3, 768, 128), F32),
            vmem((768, 384), BF16),
            vmem((768, 1024), BF16),
            vmem((768, 1024), BF16),
            vmem((1536, 1024), BF16),
            vmem((count, 384), BF16),
            vmem((count, 1024), BF16),
            vmem((count, 1024), BF16),
            vmem((384, 1024), BF16),
            vmem((384, 1024), BF16),
            vmem((ROWS, COLS, 128), BF16),
            vmem((COLS, 128), BF16),
            vmem((2, COLS, 128), BF16),
            vmem((COLS, 128), BF16),
            vmem((COLS, 128), BF16),
            vmem((COLS, 128), BF16),
            vmem((PEERS, 8, width), BF16),
            vmem((PEERS, 8, width), BF16),
            vmem((PEERS, 8, width), BF16),
            vmem((2, COLS, 128), F32),
            vmem((2, COLS, 128), F32),
            vmem((PEERS, 2, COLS, 128), BF16),
            vmem((2, COLS, 256), F32),
            vmem((2, COLS, 256), F32),
            vmem((PEERS, 2, 4, 8, 128), BF16),
            vmem((PEERS, 2, 4, 8, 128), BF16),
            dma((5,)),
            dma((5,)),
            dma((8, 4)),
            dma((8, 4)),
            dma((7, 4)),
            dma((7, 4)),
            dma((4, PEERS)),
            dma((4, PEERS)),
            dma((4,)),
            dma((4,)),
            dma((3,)),
        ],
        compiler_params=pltpu.CompilerParams(
            collective_id=0, has_side_effects=True, vmem_limit_bytes=60 * 1024 * 1024
        ),
        name="head",
    )(*operands)
    return out[None]


def solution(mesh):
    placed = (
        P(None, "seq", None, "mp"),
        P(None, "seq", None, "mp"),
        P(None, "seq", None, "mp"),
        P(None, "seq", "mp", None),
        P("mp", None),
        P(),
        P(),
        P("mp", None, None, None),
        P("mp"),
        P("mp", None, None, None),
        P("mp"),
        P(),
        P(),
    )
    return jax.shard_map(
        local, mesh=mesh, in_specs=placed, out_specs=P(None, "seq", "mp", None), check_vma=False
    )
```

```python
import jax
import jax.numpy as jnp
from jax import lax
from jax.experimental import pallas as pl
from jax.experimental.pallas import tpu as pltpu
from jax.sharding import PartitionSpec as P

EPSILON = 1e-06
MESH = pl.DeviceIdType.MESH
F32 = jnp.float32
BF16 = jnp.bfloat16
ROWS = 64
COLS = 64
PEERS = 8
LAYERS = 16
CHANNELS = 48
TAPS = (1, 2, 3, 0)
COLUMN_TAPS = (((1, None), (None, 2)), ((2, 0), (3, 1)), ((None, 3), (0, None)))


def nt(a, b):
    return lax.dot_general(a, b, (((1,), (1,)), ((), ())), preferred_element_type=F32)


def nn(a, b):
    return lax.dot_general(a, b, (((1,), (0,)), ((), ())), preferred_element_type=F32)


def tn(a, b):
    return lax.dot_general(a, b, (((0,), (0,)), ((), ())), preferred_element_type=F32)


def shifted(field):
    row = lax.broadcasted_iota(jnp.int32, field.shape, 0) & (COLS - 1)
    lane = lax.broadcasted_iota(jnp.int32, field.shape, 1) & 127
    before = jnp.where(row == 0, 0.0, pltpu.roll(field, 1, 0))
    after = jnp.where(row == COLS - 1, 0.0, pltpu.roll(field, field.shape[0] - 1, 0))
    return jnp.where(lane < CHANNELS, before, after)


def body(
    q_ref, k_ref, v_ref, resid_ref, wo_ref, gain_ref, shift_ref, w1_hbm, b1_ref, w2_hbm, b2_ref, wf_hbm, bf_ref,
    out_ref,
    w1_four, w1_raw, w1, w2_four, w2_raw, w2_tap, w2_low, w2_high, w2, wf_raw, wf_low, wf_high, low_spread, high_spread, kv, other, qb, qsend, asend, arecv, part, got, normed, halo1s, halo1r, one, halo2s, halo2r, two, tiles,
    pair_s, pair_r, right_s, right_r, left_s, left_r, mp_s, mp_r, halo_s, halo_r, load_s,
):
    s = lax.axis_index("seq")
    m = lax.axis_index("mp")
    core = lax.rem(s, 2)
    y = lax.rem(lax.div(s, 2), 2)
    z = lax.div(s, 4)

    def seq_at(zz, yy, cc):
        return zz * 4 + yy * 2 + cc

    mate = seq_at(z, y, 1 - core)
    across = seq_at(z, 1 - y, core)
    diagonal = seq_at(z, 1 - y, 1 - core)
    z_up = lax.rem(s + 4, ROWS)
    z_down = lax.rem(s + ROWS - 4, ROWS)
    row_up = lax.rem(s + 1, ROWS)
    row_down = lax.rem(s + ROWS - 1, ROWS)

    loads = [
        pltpu.make_async_copy(hbm, raw, load_s.at[i])
        for i, (hbm, raw) in enumerate(((w1_hbm, w1_four), (w2_hbm, w2_four), (wf_hbm, wf_raw)))
    ]
    for copy in loads:
        copy.start()

    barrier = pltpu.get_barrier_semaphore()
    greeted = [(mate, m), (across, m), (diagonal, m), (z_up, m), (z_down, m), (row_up, m), (row_down, m)]
    greeted += [(s, lax.rem(m + d, PEERS)) for d in range(1, PEERS)]
    for device in greeted:
        pl.semaphore_signal(barrier, inc=1, device_id=device, device_id_type=MESH)

    lane = lax.broadcasted_iota(jnp.int32, (COLS, 128), 1)
    low = lane < 64
    k = k_ref[...].astype(F32)
    v = v_ref[...].astype(F32)
    q = q_ref[...].astype(F32) * 0.125
    first = jnp.where(low, k, pltpu.roll(v, 64, 1))
    second = jnp.where(low, pltpu.roll(k, 64, 1), v)
    q_first = jnp.where(low, q, 0.0)
    q_second = jnp.where(low, pltpu.roll(q, 64, 1), 0.0)
    is_first = core == 0
    kv[s] = jnp.where(is_first, first, second).astype(BF16)
    other[...] = jnp.where(is_first, second, first).astype(BF16)
    qb[core] = jnp.where(is_first, q_first, q_second).astype(BF16)
    qsend[...] = jnp.where(is_first, q_second, q_first).astype(BF16)

    pl.semaphore_wait(barrier, len(greeted))

    def send(src, dst, ssem, rsem, device):
        return pltpu.make_async_remote_copy(
            src_ref=src, dst_ref=dst, send_sem=ssem, recv_sem=rsem, device_id=device, device_id_type=MESH
        )

    def right(t):
        block = kv.at[pl.ds(lax.rem(z - t + LAYERS, LAYERS) * 4, 4)]
        return send(block, block, right_s.at[t], right_r.at[t], (z_up, m))

    def left(t):
        block = kv.at[pl.ds(lax.rem(z + t, LAYERS) * 4, 4)]
        return send(block, block, left_s.at[t], left_r.at[t], (z_down, m))

    pair = [
        None,
        send(other, kv.at[s], pair_s.at[1], pair_r.at[1], (mate, m)),
        send(kv.at[s], kv.at[s], pair_s.at[2], pair_r.at[2], (across, m)),
        send(other, kv.at[s], pair_s.at[3], pair_r.at[3], (diagonal, m)),
        send(qsend, qb.at[core], pair_s.at[0], pair_r.at[0], (mate, m)),
    ]
    for p in (3, 2, 1, 4):
        pair[p].start()
    for p in (1, 2, 3):
        pair[p].wait_recv()
    right(0).start()
    left(0).start()
    pair[4].wait_recv()

    def attend(state, layers):
        top, total, mixed = state
        block = jnp.concatenate([kv[pl.ds(layer * 4, 4)].reshape(4 * COLS, 128) for layer in layers], axis=0)
        fresh = nt(qb[...].reshape(2 * COLS, 128), block)
        best = jnp.maximum(top, jnp.max(fresh, axis=1, keepdims=True))
        fade = jnp.exp(top - best)
        exps = jnp.exp(fresh - best)
        return (
            best,
            total * fade + jnp.sum(exps, axis=1, keepdims=True),
            mixed * fade + nn(exps.astype(BF16), block),
        )

    def arrange_one(i):
        row_tap = lax.rem(lax.div(i, 4) * 2 + lax.rem(i, 2) + 1, 4)
        side = lax.rem(lax.div(i, 2), 2) * 2
        for b in range(2):
            tap = row_tap * 4 + lax.rem(side + b + 1, 4)
            rows = pl.ds(pl.multiple_of(i * 128 + b * CHANNELS, 16), CHANNELS)
            for c in range(w1_raw.shape[0]):
                lanes = slice(c * 128, c * 128 + 128)
                w1[rows, lanes] = w1_raw[c, pl.ds(tap, CHANNELS, stride=16), :].astype(BF16)

    wide = lax.broadcasted_iota(jnp.int32, (PEERS * CHANNELS, PEERS * 128), 1)
    narrow = lax.broadcasted_iota(jnp.int32, (PEERS * CHANNELS, PEERS * 128), 0)
    within = wide & 127
    home = (wide >> 7) * CHANNELS + within
    low_spread[...] = jnp.where((narrow == home) & (within < CHANNELS), 1.0, 0.0).astype(BF16)
    high_spread[...] = jnp.where(
        (narrow == home - CHANNELS) & (within >= CHANNELS) & (within < 2 * CHANNELS), 1.0, 0.0
    ).astype(BF16)
    bias1 = twice(b1_ref[...])
    bias2 = twice(b2_ref[...])
    for copy in loads:
        copy.wait()

    def flatten(four, raw, first, last):
        def rows_of(e, carry):
            rows = pl.ds(pl.multiple_of(e * 32, 32), 32)
            flat = four[pl.ds(e * 2, 2)].astype(F32).reshape(32, four.shape[-1])
            for c in range(raw.shape[0]):
                raw[c, rows, :] = flat[:, c * 128 : c * 128 + 128]
            return carry

        lax.fori_loop(first, last, rows_of, 0)

    start = (
        jnp.full((2 * COLS, 1), -jnp.inf, F32),
        jnp.zeros((2 * COLS, 1), F32),
        jnp.zeros((2 * COLS, 128), F32),
    )
    state = attend(start, [z])
    for i in range(8):
        w1[i * 128 + 2 * CHANNELS : i * 128 + 128, :] = jnp.zeros((32, w1.shape[1]), BF16)
    for i in range(12):
        w2[i * 128 + 2 * CHANNELS : i * 128 + 128, :] = jnp.zeros((32, w2.shape[1]), BF16)

    def ring(t, state):
        right(t - 1).wait_recv()
        right(t).start()
        left(t - 1).wait_recv()
        left(t).start()
        return attend(state, [lax.rem(z - t + LAYERS, LAYERS), lax.rem(z + t, LAYERS)])

    def ring_flatten(t, state):
        state = ring(t, state)
        flatten(w1_four, w1_raw, (t - 1) * 8, t * 8)
        return state

    def ring_arrange(t, state):
        state = ring(t, state)
        arrange_one((t - 4) * 2)
        arrange_one((t - 4) * 2 + 1)
        return state

    state = lax.fori_loop(1, 4, ring_flatten, state)
    state = lax.fori_loop(4, 7, ring_arrange, state)
    right(6).wait_recv()
    right(7).start()
    left(6).wait_recv()
    state = attend(state, [lax.rem(z + 9, LAYERS), lax.rem(z + 7, LAYERS)])
    arrange_one(6)
    arrange_one(7)
    right(7).wait_recv()
    top, total, mixed = attend(state, [lax.rem(z + 8, LAYERS)])
    attended = mixed / total
    placed = jnp.where(is_first, jnp.where(low, pltpu.roll(attended[:COLS], 64, 1), 0.0), jnp.where(low, 0.0, attended[:COLS]))
    placed_too = jnp.where(is_first, jnp.where(low, pltpu.roll(attended[COLS:], 64, 1), 0.0), jnp.where(low, 0.0, attended[COLS:]))
    asend[...] = jnp.where(is_first, placed_too, placed).astype(BF16)
    swap = send(asend, arecv, pair_s.at[4], pair_r.at[4], (mate, m))
    swap.start()
    mine = jnp.where(is_first, placed, placed_too).astype(BF16)
    swap.wait_recv()
    rows = (mine.astype(F32) + arecv[...].astype(F32)).astype(BF16)

    def exchange(phase, source, target):
        copies = []
        for d in range(1, PEERS):
            peer = lax.rem(m + d, PEERS)
            copies.append(send(source(peer), target, mp_s.at[phase, d], mp_r.at[phase, d], (s, peer)))
        for copy in copies:
            copy.start()
        return copies

    def arrived(copies):
        for copy in copies:
            copy.wait_recv()

    part[...] = nn(rows, wo_ref[...]).reshape(PEERS, 8, -1).astype(BF16)
    sums = exchange(0, lambda peer: part.at[peer], got.at[m])
    stream = resid_ref[...].astype(F32) + part[m].astype(F32)
    got[m] = jnp.zeros(got.shape[1:], BF16)
    flatten(w2_four, w2_raw, 0, CHANNELS // 2)
    for tap in range(16):
        for c in range(w2_raw.shape[0]):
            rows = w2_raw[c, pl.ds(tap, CHANNELS, stride=16), :]
            w2_tap[tap * CHANNELS : (tap + 1) * CHANNELS, c * 128 : c * 128 + 128] = rows.astype(BF16)
    arrived(sums)
    for j in range(PEERS):
        stream = stream + got[j].astype(F32)
    center = jnp.mean(stream, axis=1, keepdims=True)
    apart = stream - center
    variance = jnp.mean(apart * apart, axis=1, keepdims=True)
    normed[m] = (apart * lax.rsqrt(variance + EPSILON) * gain_ref[...][None] + shift_ref[...][None]).astype(BF16)
    norms = exchange(1, lambda peer: normed.at[m], normed.at[m])
    w2_low[...] = nn(w2_tap[...], low_spread[...]).astype(BF16)
    w2_high[...] = nn(w2_tap[...], high_spread[...]).astype(BF16)
    arrived(norms)
    tokens = normed[...].astype(F32).reshape(COLS, -1).astype(BF16)

    def first_block(i):
        return nt(tokens, w1[pl.ds(i * 256, 256), :])

    crossing = first_block(2) + shifted(first_block(3))
    halo1s[0] = crossing[:, :128]
    halo1s[1] = crossing[:, 128:]
    to_up = send(halo1s.at[0], halo1r.at[0], halo_s.at[0], halo_r.at[0], (row_up, m))
    to_down = send(halo1s.at[1], halo1r.at[1], halo_s.at[1], halo_r.at[1], (row_down, m))
    to_up.start()
    to_down.start()
    inside = first_block(0) + shifted(first_block(1))
    to_up.wait_recv()
    to_down.wait_recv()
    upper = inside[:, :128] + jnp.where(s > 0, halo1r[0], 0.0)
    lower = inside[:, 128:] + jnp.where(s < ROWS - 1, halo1r[1], 0.0)
    one[m, 0] = jnp.maximum(upper + bias1, 0.0).astype(BF16)
    one[m, 1] = jnp.maximum(lower + bias1, 0.0).astype(BF16)
    ones = exchange(2, lambda peer: one.at[m], one.at[m])
    for i in range(4):
        for n in range(3):
            base = i * 384 + n * 128
            for g in range(2):
                blocks = [
                    spread[(TAPS[i] * 4 + t) * CHANNELS : (TAPS[i] * 4 + t + 1) * CHANNELS, :]
                    for spread, t in zip((w2_low, w2_high), COLUMN_TAPS[n][g])
                    if t is not None
                ]
                w2[base + g * CHANNELS : base + (g + 1) * CHANNELS, :] = sum(blocks[1:], blocks[0])
    wf_low[...] = nn(wf_raw[...], low_spread[...]).astype(BF16)
    wf_high[...] = nn(wf_raw[...], high_spread[...]).astype(BF16)
    arrived(ones)
    cells = jnp.concatenate([one[j].reshape(2 * COLS, 128) for j in range(PEERS)], axis=1)

    def second_block(i):
        product = nt(cells, w2[pl.ds(i * 384, 384), :])
        return product[:, :128] + shifted(product[:, 256:]), product[:, 128:256]

    down_first, down_second = second_block(2)
    up_first, up_second = second_block(3)
    halo2s[0, :, :128] = down_first[COLS:]
    halo2s[0, :, 128:] = down_second[COLS:]
    halo2s[1, :, :128] = up_first[:COLS]
    halo2s[1, :, 128:] = up_second[:COLS]
    to_up2 = send(halo2s.at[0], halo2r.at[0], halo_s.at[2], halo_r.at[2], (row_up, m))
    to_down2 = send(halo2s.at[1], halo2r.at[1], halo_s.at[3], halo_r.at[3], (row_down, m))
    to_up2.start()
    to_down2.start()
    even_first, even_second = second_block(0)
    odd_first, odd_second = second_block(1)
    halves = [
        [even_first[:COLS], even_second[:COLS]],
        [odd_first[:COLS] + up_first[COLS:], odd_second[:COLS] + up_second[COLS:]],
        [even_first[COLS:] + down_first[:COLS], even_second[COLS:] + down_second[:COLS]],
        [odd_first[COLS:], odd_second[COLS:]],
    ]
    to_up2.wait_recv()
    to_down2.wait_recv()
    for h in range(2):
        lanes = slice(h * 128, h * 128 + 128)
        halves[0][h] = halves[0][h] + jnp.where(s > 0, halo2r[0, :, lanes], 0.0)
        halves[3][h] = halves[3][h] + jnp.where(s < ROWS - 1, halo2r[1, :, lanes], 0.0)
        for r in range(4):
            block = jnp.maximum(halves[r][h] + bias2, 0.0)
            two[:, h, r] = block.reshape(PEERS, 8, 128).astype(BF16)
    tiles[m] = two[m]
    twos = exchange(3, lambda peer: two.at[peer], tiles.at[m])
    arrived(twos)
    positions = jnp.concatenate(
        [tiles[j].astype(F32).reshape(64, 128).astype(BF16) for j in range(PEERS)], axis=1
    )
    apart_maps = [(nt(positions, weight[...]) + bf_ref[...][None]).astype(BF16) for weight in (wf_low, wf_high)]
    maps = jnp.concatenate(apart_maps, axis=0)
    place = lax.broadcasted_iota(jnp.int32, (128, 128), 0)
    source = (
        ((place >> 1) & 1) * 64
        + ((place ^ (place >> 1)) & 1) * 32
        + (place >> 5) * 8
        + ((place >> 2) & 7)
    )
    order = jnp.where(lax.broadcasted_iota(jnp.int32, (128, 128), 1) == source, 1.0, 0.0).astype(BF16)
    out_ref[...] = nn(order, maps).astype(BF16).reshape(out_ref.shape)

    for p in (1, 2, 3, 4):
        pair[p].wait_send()
    swap.wait_send()

    def sent(t, carry):
        right(t).wait_send()
        left(t).wait_send()
        return carry

    lax.fori_loop(0, 7, sent, 0)
    right(7).wait_send()
    for copy in sums + norms + ones + twos + [to_up, to_down, to_up2, to_down2]:
        copy.wait_send()


def twice(bias):
    lane = lax.broadcasted_iota(jnp.int32, (CHANNELS, 128), 1)
    home = jnp.where(lane < CHANNELS, lane, lane - CHANNELS)
    spread = jnp.where(lax.broadcasted_iota(jnp.int32, (CHANNELS, 128), 0) == home, 1.0, 0.0)
    return jnp.dot(jnp.broadcast_to(bias[None], (8, CHANNELS)), spread, precision=lax.Precision.HIGHEST)[:1]


def local(
    query, keys, values, resid, out_weight, norm_gain, norm_bias,
    deconv1_weight, deconv1_bias, deconv2_weight, deconv2_bias, final_weight, final_bias,
):
    width = resid.shape[-1]
    count = final_weight.shape[-1]
    operands = (
        query.reshape(COLS, 128),
        keys.reshape(COLS, 128),
        values.reshape(COLS, 128),
        resid.reshape(8, width),
        out_weight,
        norm_gain,
        norm_bias,
        deconv1_weight,
        deconv1_bias,
        deconv2_weight,
        deconv2_bias,
        final_weight.T,
        final_bias,
    )
    dma = pltpu.SemaphoreType.DMA
    vmem = pltpu.VMEM
    out = pl.pallas_call(
        body,
        out_shape=jax.ShapeDtypeStruct((4, 32, count), BF16),
        in_specs=[
            pl.BlockSpec(memory_space=pl.ANY if i in (7, 9, 11) else pltpu.VMEM) for i in range(len(operands))
        ],
        out_specs=pl.BlockSpec(memory_space=pltpu.VMEM),
        scratch_shapes=[
            vmem((CHANNELS, 4, 4, width), BF16),
            vmem((width // 128, 768, 128), F32),
            vmem((1024, width), BF16),
            vmem((CHANNELS, 4, 4, 384), BF16),
            vmem((3, 768, 128), F32),
            vmem((768, 384), BF16),
            vmem((768, 1024), BF16),
            vmem((768, 1024), BF16),
            vmem((1536, 1024), BF16),
            vmem((count, 384), BF16),
            vmem((count, 1024), BF16),
            vmem((count, 1024), BF16),
            vmem((384, 1024), BF16),
            vmem((384, 1024), BF16),
            vmem((ROWS, COLS, 128), BF16),
            vmem((COLS, 128), BF16),
            vmem((2, COLS, 128), BF16),
            vmem((COLS, 128), BF16),
            vmem((COLS, 128), BF16),
            vmem((COLS, 128), BF16),
            vmem((PEERS, 8, width), BF16),
            vmem((PEERS, 8, width), BF16),
            vmem((PEERS, 8, width), BF16),
            vmem((2, COLS, 128), F32),
            vmem((2, COLS, 128), F32),
            vmem((PEERS, 2, COLS, 128), BF16),
            vmem((2, COLS, 256), F32),
            vmem((2, COLS, 256), F32),
            vmem((PEERS, 2, 4, 8, 128), BF16),
            vmem((PEERS, 2, 4, 8, 128), BF16),
            dma((5,)),
            dma((5,)),
            dma((8,)),
            dma((8,)),
            dma((7,)),
            dma((7,)),
            dma((4, PEERS)),
            dma((4, PEERS)),
            dma((4,)),
            dma((4,)),
            dma((3,)),
        ],
        compiler_params=pltpu.CompilerParams(
            collective_id=0, has_side_effects=True, vmem_limit_bytes=60 * 1024 * 1024
        ),
        name="head",
    )(*operands)
    return out[None]


def solution(mesh):
    placed = (
        P(None, "seq", None, "mp"),
        P(None, "seq", None, "mp"),
        P(None, "seq", None, "mp"),
        P(None, "seq", "mp", None),
        P("mp", None),
        P(),
        P(),
        P("mp", None, None, None),
        P("mp"),
        P("mp", None, None, None),
        P("mp"),
        P(),
        P(),
    )
    return jax.shard_map(
        local, mesh=mesh, in_specs=placed, out_specs=P(None, "seq", "mp", None), check_vma=False
    )
```

```python
import jax
import jax.numpy as jnp
from jax import lax
from jax.experimental import pallas as pl
from jax.experimental.pallas import tpu as pltpu
from jax.sharding import PartitionSpec as P

EPSILON = 1e-06
MESH = pl.DeviceIdType.MESH
F32 = jnp.float32
BF16 = jnp.bfloat16
ROWS = 64
COLS = 64
PEERS = 8
LAYERS = 16
CHANNELS = 48
TAPS = (1, 2, 3, 0)
COLUMN_TAPS = (((1, None), (None, 2)), ((2, 0), (3, 1)), ((None, 3), (0, None)))


def nt(a, b):
    return lax.dot_general(a, b, (((1,), (1,)), ((), ())), preferred_element_type=F32)


def nn(a, b):
    return lax.dot_general(a, b, (((1,), (0,)), ((), ())), preferred_element_type=F32)


def tn(a, b):
    return lax.dot_general(a, b, (((0,), (0,)), ((), ())), preferred_element_type=F32)


def shifted(field):
    row = lax.broadcasted_iota(jnp.int32, field.shape, 0) & (COLS - 1)
    lane = lax.broadcasted_iota(jnp.int32, field.shape, 1) & 127
    before = jnp.where(row == 0, 0.0, pltpu.roll(field, 1, 0))
    after = jnp.where(row == COLS - 1, 0.0, pltpu.roll(field, field.shape[0] - 1, 0))
    return jnp.where(lane < CHANNELS, before, after)


def body(
    q_ref, k_ref, v_ref, resid_ref, wo_ref, gain_ref, shift_ref, w1_hbm, b1_ref, w2_hbm, b2_ref, wf_hbm, bf_ref,
    out_ref,
    w1_four, w1_raw, w1, w2_four, w2_raw, w2_tap, w2_low, w2_high, w2, wf_raw, wf_low, wf_high, low_spread, high_spread, kv, other, qb, qsend, asend, arecv, part, got, normed, halo1s, halo1r, one, halo2s, halo2r, two, tiles,
    pair_s, pair_r, right_s, right_r, left_s, left_r, mp_s, mp_r, halo_s, halo_r, load_s,
):
    s = lax.axis_index("seq")
    m = lax.axis_index("mp")
    core = lax.rem(s, 2)
    y = lax.rem(lax.div(s, 2), 2)
    z = lax.div(s, 4)

    def seq_at(zz, yy, cc):
        return zz * 4 + yy * 2 + cc

    mate = seq_at(z, y, 1 - core)
    across = seq_at(z, 1 - y, core)
    diagonal = seq_at(z, 1 - y, 1 - core)
    z_up = lax.rem(s + 4, ROWS)
    z_down = lax.rem(s + ROWS - 4, ROWS)
    row_up = lax.rem(s + 1, ROWS)
    row_down = lax.rem(s + ROWS - 1, ROWS)

    loads = [
        pltpu.make_async_copy(hbm, raw, load_s.at[i])
        for i, (hbm, raw) in enumerate(((w1_hbm, w1_four), (w2_hbm, w2_four), (wf_hbm, wf_raw)))
    ]
    for copy in loads:
        copy.start()

    barrier = pltpu.get_barrier_semaphore()
    greeted = [(mate, m), (across, m), (diagonal, m), (z_up, m), (z_down, m), (row_up, m), (row_down, m)]
    greeted += [(s, lax.rem(m + d, PEERS)) for d in range(1, PEERS)]
    for device in greeted:
        pl.semaphore_signal(barrier, inc=1, device_id=device, device_id_type=MESH)

    lane = lax.broadcasted_iota(jnp.int32, (COLS, 128), 1)
    low = lane < 64
    k = k_ref[...].astype(F32)
    v = v_ref[...].astype(F32)
    q = q_ref[...].astype(F32) * 0.125
    first = jnp.where(low, k, pltpu.roll(v, 64, 1))
    second = jnp.where(low, pltpu.roll(k, 64, 1), v)
    q_first = jnp.where(low, q, 0.0)
    q_second = jnp.where(low, pltpu.roll(q, 64, 1), 0.0)
    is_first = core == 0
    kv[s] = jnp.where(is_first, first, second).astype(BF16)
    other[...] = jnp.where(is_first, second, first).astype(BF16)
    qb[core] = jnp.where(is_first, q_first, q_second).astype(BF16)
    qsend[...] = jnp.where(is_first, q_second, q_first).astype(BF16)

    wide = lax.broadcasted_iota(jnp.int32, (PEERS * CHANNELS, PEERS * 128), 1)
    narrow = lax.broadcasted_iota(jnp.int32, (PEERS * CHANNELS, PEERS * 128), 0)
    within = wide & 127
    home = (wide >> 7) * CHANNELS + within
    low_spread[...] = jnp.where((narrow == home) & (within < CHANNELS), 1.0, 0.0).astype(BF16)
    high_spread[...] = jnp.where(
        (narrow == home - CHANNELS) & (within >= CHANNELS) & (within < 2 * CHANNELS), 1.0, 0.0
    ).astype(BF16)
    pl.semaphore_wait(barrier, len(greeted))

    def send(src, dst, ssem, rsem, device):
        return pltpu.make_async_remote_copy(
            src_ref=src, dst_ref=dst, send_sem=ssem, recv_sem=rsem, device_id=device, device_id_type=MESH
        )

    def piece(layer, p):
        yy = y if p < 2 else 1 - y
        cc = core if p % 2 == 0 else 1 - core
        return seq_at(layer, yy, cc)

    def right(t, p):
        block = kv.at[piece(lax.rem(z - t + LAYERS, LAYERS), p)]
        return send(block, block, right_s.at[t, p], right_r.at[t, p], (z_up, m))

    def left(t, p):
        block = kv.at[piece(lax.rem(z + t, LAYERS), p)]
        return send(block, block, left_s.at[t, p], left_r.at[t, p], (z_down, m))

    right(0, 0).start()
    left(0, 0).start()
    pair = [
        None,
        send(other, kv.at[s], pair_s.at[1], pair_r.at[1], (mate, m)),
        send(kv.at[s], kv.at[s], pair_s.at[2], pair_r.at[2], (across, m)),
        send(other, kv.at[s], pair_s.at[3], pair_r.at[3], (diagonal, m)),
        send(qsend, qb.at[core], pair_s.at[0], pair_r.at[0], (mate, m)),
    ]
    for p in (2, 1, 4, 3):
        pair[p].start()
    for p in (1, 2, 3):
        pair[p].wait_recv()
        right(0, p).start()
        left(0, p).start()
    pair[4].wait_recv()

    def attend(state, layers):
        top, total, mixed = state
        block = jnp.concatenate([kv[pl.ds(layer * 4, 4)].reshape(4 * COLS, 128) for layer in layers], axis=0)
        fresh = nt(qb[...].reshape(2 * COLS, 128), block)
        best = jnp.maximum(top, jnp.max(fresh, axis=1, keepdims=True))
        fade = jnp.exp(top - best)
        exps = jnp.exp(fresh - best)
        return (
            best,
            total * fade + jnp.sum(exps, axis=1, keepdims=True),
            mixed * fade + nn(exps.astype(BF16), block),
        )

    def arrange_one(i):
        row_tap = lax.rem(lax.div(i, 4) * 2 + lax.rem(i, 2) + 1, 4)
        side = lax.rem(lax.div(i, 2), 2) * 2
        for b in range(2):
            tap = row_tap * 4 + lax.rem(side + b + 1, 4)
            rows = pl.ds(pl.multiple_of(i * 128 + b * CHANNELS, 16), CHANNELS)
            for c in range(w1_raw.shape[0]):
                lanes = slice(c * 128, c * 128 + 128)
                w1[rows, lanes] = w1_raw[c, pl.ds(tap, CHANNELS, stride=16), :].astype(BF16)

    for copy in loads:
        copy.wait()

    def flatten(four, raw, first, last):
        def rows_of(e, carry):
            rows = pl.ds(pl.multiple_of(e * 32, 32), 32)
            flat = four[pl.ds(e * 2, 2)].astype(F32).reshape(32, four.shape[-1])
            for c in range(raw.shape[0]):
                raw[c, rows, :] = flat[:, c * 128 : c * 128 + 128]
            return carry

        lax.fori_loop(first, last, rows_of, 0)

    start = (
        jnp.full((2 * COLS, 1), -jnp.inf, F32),
        jnp.zeros((2 * COLS, 1), F32),
        jnp.zeros((2 * COLS, 128), F32),
    )
    state = attend(start, [z])

    def ring(t, state):
        for p in range(4):
            right(t - 1, p).wait_recv()
            right(t, p).start()
            left(t - 1, p).wait_recv()
            left(t, p).start()
        return attend(state, [lax.rem(z - t + LAYERS, LAYERS), lax.rem(z + t, LAYERS)])

    def ring_flatten(t, state):
        state = ring(t, state)
        flatten(w1_four, w1_raw, (t - 1) * 8, t * 8)
        return state

    def ring_arrange(t, state):
        state = ring(t, state)
        arrange_one((t - 4) * 2)
        arrange_one((t - 4) * 2 + 1)
        return state

    state = lax.fori_loop(1, 4, ring_flatten, state)
    state = lax.fori_loop(4, 7, ring_arrange, state)
    for p in range(4):
        right(6, p).wait_recv()
        right(7, p).start()
    for p in range(4):
        left(6, p).wait_recv()
    state = attend(state, [lax.rem(z + 9, LAYERS), lax.rem(z + 7, LAYERS)])
    bias1 = twice(b1_ref[...])
    bias2 = twice(b2_ref[...])
    for i in range(8):
        w1[i * 128 + 2 * CHANNELS : i * 128 + 128, :] = jnp.zeros((32, w1.shape[1]), BF16)
    for i in range(12):
        w2[i * 128 + 2 * CHANNELS : i * 128 + 128, :] = jnp.zeros((32, w2.shape[1]), BF16)
    arrange_one(6)
    arrange_one(7)
    for p in range(4):
        right(7, p).wait_recv()
    top, total, mixed = attend(state, [lax.rem(z + 8, LAYERS)])
    attended = mixed / total
    placed = jnp.where(is_first, jnp.where(low, pltpu.roll(attended[:COLS], 64, 1), 0.0), jnp.where(low, 0.0, attended[:COLS]))
    placed_too = jnp.where(is_first, jnp.where(low, pltpu.roll(attended[COLS:], 64, 1), 0.0), jnp.where(low, 0.0, attended[COLS:]))
    asend[...] = jnp.where(is_first, placed_too, placed).astype(BF16)
    swap = send(asend, arecv, pair_s.at[4], pair_r.at[4], (mate, m))
    swap.start()
    mine = jnp.where(is_first, placed, placed_too).astype(BF16)
    swap.wait_recv()
    rows = (mine.astype(F32) + arecv[...].astype(F32)).astype(BF16)

    def exchange(phase, source, target):
        copies = []
        for d in range(1, PEERS):
            peer = lax.rem(m + d, PEERS)
            copies.append(send(source(peer), target, mp_s.at[phase, d], mp_r.at[phase, d], (s, peer)))
        for copy in copies:
            copy.start()
        return copies

    def arrived(copies):
        for copy in copies:
            copy.wait_recv()

    part[...] = nn(rows, wo_ref[...]).reshape(PEERS, 8, -1).astype(BF16)
    sums = exchange(0, lambda peer: part.at[peer], got.at[m])
    stream = resid_ref[...].astype(F32) + part[m].astype(F32)
    got[m] = jnp.zeros(got.shape[1:], BF16)
    flatten(w2_four, w2_raw, 0, CHANNELS // 2)
    for tap in range(16):
        for c in range(w2_raw.shape[0]):
            rows = w2_raw[c, pl.ds(tap, CHANNELS, stride=16), :]
            w2_tap[tap * CHANNELS : (tap + 1) * CHANNELS, c * 128 : c * 128 + 128] = rows.astype(BF16)
    arrived(sums)
    for j in range(PEERS):
        stream = stream + got[j].astype(F32)
    center = jnp.mean(stream, axis=1, keepdims=True)
    apart = stream - center
    variance = jnp.mean(apart * apart, axis=1, keepdims=True)
    normed[m] = (apart * lax.rsqrt(variance + EPSILON) * gain_ref[...][None] + shift_ref[...][None]).astype(BF16)
    norms = exchange(1, lambda peer: normed.at[m], normed.at[m])
    w2_low[...] = nn(w2_tap[...], low_spread[...]).astype(BF16)
    w2_high[...] = nn(w2_tap[...], high_spread[...]).astype(BF16)
    arrived(norms)
    tokens = normed[...].astype(F32).reshape(COLS, -1).astype(BF16)

    def first_block(i):
        return nt(tokens, w1[pl.ds(i * 256, 256), :])

    crossing = first_block(2) + shifted(first_block(3))
    halo1s[0] = crossing[:, :128]
    halo1s[1] = crossing[:, 128:]
    to_up = send(halo1s.at[0], halo1r.at[0], halo_s.at[0], halo_r.at[0], (row_up, m))
    to_down = send(halo1s.at[1], halo1r.at[1], halo_s.at[1], halo_r.at[1], (row_down, m))
    to_up.start()
    to_down.start()
    inside = first_block(0) + shifted(first_block(1))
    to_up.wait_recv()
    to_down.wait_recv()
    upper = inside[:, :128] + jnp.where(s > 0, halo1r[0], 0.0)
    lower = inside[:, 128:] + jnp.where(s < ROWS - 1, halo1r[1], 0.0)
    one[m, 0] = jnp.maximum(upper + bias1, 0.0).astype(BF16)
    one[m, 1] = jnp.maximum(lower + bias1, 0.0).astype(BF16)
    ones = exchange(2, lambda peer: one.at[m], one.at[m])
    for i in range(4):
        for n in range(3):
            base = i * 384 + n * 128
            for g in range(2):
                blocks = [
                    spread[(TAPS[i] * 4 + t) * CHANNELS : (TAPS[i] * 4 + t + 1) * CHANNELS, :]
                    for spread, t in zip((w2_low, w2_high), COLUMN_TAPS[n][g])
                    if t is not None
                ]
                w2[base + g * CHANNELS : base + (g + 1) * CHANNELS, :] = sum(blocks[1:], blocks[0])
    wf_low[...] = nn(wf_raw[...], low_spread[...]).astype(BF16)
    wf_high[...] = nn(wf_raw[...], high_spread[...]).astype(BF16)
    arrived(ones)
    cells = jnp.concatenate([one[j].reshape(2 * COLS, 128) for j in range(PEERS)], axis=1)

    def second_block(i):
        product = nt(cells, w2[pl.ds(i * 384, 384), :])
        return product[:, :128] + shifted(product[:, 256:]), product[:, 128:256]

    down_first, down_second = second_block(2)
    up_first, up_second = second_block(3)
    halo2s[0, :, :128] = down_first[COLS:]
    halo2s[0, :, 128:] = down_second[COLS:]
    halo2s[1, :, :128] = up_first[:COLS]
    halo2s[1, :, 128:] = up_second[:COLS]
    to_up2 = send(halo2s.at[0], halo2r.at[0], halo_s.at[2], halo_r.at[2], (row_up, m))
    to_down2 = send(halo2s.at[1], halo2r.at[1], halo_s.at[3], halo_r.at[3], (row_down, m))
    to_up2.start()
    to_down2.start()
    even_first, even_second = second_block(0)
    odd_first, odd_second = second_block(1)
    halves = [
        [even_first[:COLS], even_second[:COLS]],
        [odd_first[:COLS] + up_first[COLS:], odd_second[:COLS] + up_second[COLS:]],
        [even_first[COLS:] + down_first[:COLS], even_second[COLS:] + down_second[:COLS]],
        [odd_first[COLS:], odd_second[COLS:]],
    ]
    to_up2.wait_recv()
    to_down2.wait_recv()
    for h in range(2):
        lanes = slice(h * 128, h * 128 + 128)
        halves[0][h] = halves[0][h] + jnp.where(s > 0, halo2r[0, :, lanes], 0.0)
        halves[3][h] = halves[3][h] + jnp.where(s < ROWS - 1, halo2r[1, :, lanes], 0.0)
        for r in range(4):
            block = jnp.maximum(halves[r][h] + bias2, 0.0)
            two[:, h, r] = block.reshape(PEERS, 8, 128).astype(BF16)
    tiles[m] = two[m]
    twos = exchange(3, lambda peer: two.at[peer], tiles.at[m])
    arrived(twos)
    positions = jnp.concatenate(
        [tiles[j].astype(F32).reshape(64, 128).astype(BF16) for j in range(PEERS)], axis=1
    )
    apart_maps = [(nt(positions, weight[...]) + bf_ref[...][None]).astype(BF16) for weight in (wf_low, wf_high)]
    maps = jnp.concatenate(apart_maps, axis=0)
    place = lax.broadcasted_iota(jnp.int32, (128, 128), 0)
    source = (
        ((place >> 1) & 1) * 64
        + ((place ^ (place >> 1)) & 1) * 32
        + (place >> 5) * 8
        + ((place >> 2) & 7)
    )
    order = jnp.where(lax.broadcasted_iota(jnp.int32, (128, 128), 1) == source, 1.0, 0.0).astype(BF16)
    out_ref[...] = nn(order, maps).astype(BF16).reshape(out_ref.shape)

    for p in (1, 2, 3, 4):
        pair[p].wait_send()
    swap.wait_send()

    def sent(t, carry):
        for p in range(4):
            right(t, p).wait_send()
            left(t, p).wait_send()
        return carry

    lax.fori_loop(0, 7, sent, 0)
    for p in range(4):
        right(7, p).wait_send()
    for copy in sums + norms + ones + twos + [to_up, to_down, to_up2, to_down2]:
        copy.wait_send()


def twice(bias):
    lane = lax.broadcasted_iota(jnp.int32, (CHANNELS, 128), 1)
    home = jnp.where(lane < CHANNELS, lane, lane - CHANNELS)
    spread = jnp.where(lax.broadcasted_iota(jnp.int32, (CHANNELS, 128), 0) == home, 1.0, 0.0)
    return jnp.dot(jnp.broadcast_to(bias[None], (8, CHANNELS)), spread, precision=lax.Precision.HIGHEST)[:1]


def local(
    query, keys, values, resid, out_weight, norm_gain, norm_bias,
    deconv1_weight, deconv1_bias, deconv2_weight, deconv2_bias, final_weight, final_bias,
):
    width = resid.shape[-1]
    count = final_weight.shape[-1]
    operands = (
        query.reshape(COLS, 128),
        keys.reshape(COLS, 128),
        values.reshape(COLS, 128),
        resid.reshape(8, width),
        out_weight,
        norm_gain,
        norm_bias,
        deconv1_weight,
        deconv1_bias,
        deconv2_weight,
        deconv2_bias,
        final_weight.T,
        final_bias,
    )
    dma = pltpu.SemaphoreType.DMA
    vmem = pltpu.VMEM
    out = pl.pallas_call(
        body,
        out_shape=jax.ShapeDtypeStruct((4, 32, count), BF16),
        in_specs=[
            pl.BlockSpec(memory_space=pl.ANY if i in (7, 9, 11) else pltpu.VMEM) for i in range(len(operands))
        ],
        out_specs=pl.BlockSpec(memory_space=pltpu.VMEM),
        scratch_shapes=[
            vmem((CHANNELS, 4, 4, width), BF16),
            vmem((width // 128, 768, 128), F32),
            vmem((1024, width), BF16),
            vmem((CHANNELS, 4, 4, 384), BF16),
            vmem((3, 768, 128), F32),
            vmem((768, 384), BF16),
            vmem((768, 1024), BF16),
            vmem((768, 1024), BF16),
            vmem((1536, 1024), BF16),
            vmem((count, 384), BF16),
            vmem((count, 1024), BF16),
            vmem((count, 1024), BF16),
            vmem((384, 1024), BF16),
            vmem((384, 1024), BF16),
            vmem((ROWS, COLS, 128), BF16),
            vmem((COLS, 128), BF16),
            vmem((2, COLS, 128), BF16),
            vmem((COLS, 128), BF16),
            vmem((COLS, 128), BF16),
            vmem((COLS, 128), BF16),
            vmem((PEERS, 8, width), BF16),
            vmem((PEERS, 8, width), BF16),
            vmem((PEERS, 8, width), BF16),
            vmem((2, COLS, 128), F32),
            vmem((2, COLS, 128), F32),
            vmem((PEERS, 2, COLS, 128), BF16),
            vmem((2, COLS, 256), F32),
            vmem((2, COLS, 256), F32),
            vmem((PEERS, 2, 4, 8, 128), BF16),
            vmem((PEERS, 2, 4, 8, 128), BF16),
            dma((5,)),
            dma((5,)),
            dma((8, 4)),
            dma((8, 4)),
            dma((7, 4)),
            dma((7, 4)),
            dma((4, PEERS)),
            dma((4, PEERS)),
            dma((4,)),
            dma((4,)),
            dma((3,)),
        ],
        compiler_params=pltpu.CompilerParams(
            collective_id=0, has_side_effects=True, vmem_limit_bytes=60 * 1024 * 1024
        ),
        name="head",
    )(*operands)
    return out[None]


def solution(mesh):
    placed = (
        P(None, "seq", None, "mp"),
        P(None, "seq", None, "mp"),
        P(None, "seq", None, "mp"),
        P(None, "seq", "mp", None),
        P("mp", None),
        P(),
        P(),
        P("mp", None, None, None),
        P("mp"),
        P("mp", None, None, None),
        P("mp"),
        P(),
        P(),
    )
    return jax.shard_map(
        local, mesh=mesh, in_specs=placed, out_specs=P(None, "seq", "mp", None), check_vma=False
    )
```
